1024 devices in a mesh: dp: 8 (over y), node: 16 (over z), local: 8 (over x, core).
Axes of the slice: x: 4, y: 8, z: 16, core: 2. Of those that a mesh axis runs over, the one named last changes fastest.
Arguments:
- tokens: bfloat16 [16384, 2048], P(('dp', 'node', 'local')), parts along dimension 0, may hold values from -6 to 6
- cotangent: bfloat16 [16384, 2048], P(('dp', 'node', 'local')), parts along dimension 0, may hold values from -6 to 6
- expert_ids: int32 [16384, 8], P(('dp', 'node', 'local')), parts along dimension 0, may hold values from 0 to 127, all different within a row; in each aligned block of 16 rows (0 to 15, 16 to 31, ...) at most 2 rows name the same one
- combine: float32 [16384, 8], P(('dp', 'node', 'local')), parts along dimension 0, may hold values from 0.05 to 0.3
- w_gate_up: bfloat16 [128, 2048, 768], P(('node', 'local')), may hold values from -0.125 to 0.125
- w_down: bfloat16 [128, 384, 2048], P(('node', 'local')), may hold values from -0.3125 to 0.3125
Outputs:
- mixed: bfloat16 [16384, 2048], P(('dp', 'node', 'local')), parts along dimension 0
- grad_tokens: bfloat16 [16384, 2048], P(('dp', 'node', 'local')), parts along dimension 0
- grad_combine: float32 [16384, 8], P(('dp', 'node', 'local')), parts along dimension 0
The draws below stay inside these ranges and needn't reach their ends.
There are 8 independent parts, one for each index of `dp`. The reference program is written for one: setup_inputs(seed, part) draws one part's arguments, and reference() takes and returns one part's arrays. A program takes and returns all parts, laid end to end along the dimension named above; an argument that names none is the same for every part. Nothing has to cross between parts.
Inputs may be any that keep to these rules, and one draw needn't show every extreme that they name: `expert_ids`: each row names 8 different experts. Among the rows of one device no expert is named more than 2 times, a bound that some block reaches.
All inputs are finite; a program needn't handle non-finite values.
Results may differ from the reference program's by a relative error of at most 0.012.
Values may be sent and summed in bfloat16 or wider, within the bound.
No kernel may reach another device: no remote copies, remote signals or barrier semaphores. Data moves between devices by JAX's collectives and lax.ppermute only.
A program may use at most 32 MiB of HBM per device.

```python
import math
import jax
import jax.numpy as jnp
import numpy as np
from jax import lax

D = 2048
FF = 384
TOP = 8
TOK_DEV = 16
EXPERTS = 128
CAP = 2
TOKENS = 2048
N_NODE = 16
N_LOCAL = 8


def levels(stream_key, shape, pieces, least, largest):
    def one(position, blocks):
        heights = jax.random.uniform(jax.random.fold_in(jax.random.fold_in(stream_key, 6), position), (blocks,), jnp.float32, least / len(pieces), largest / len(pieces))
        return jnp.repeat(jnp.exp(heights), shape[position] // blocks).reshape((-1,) + (1,) * (len(shape) - position - 1))

    factor_of = one(*pieces[0])
    for cut in pieces[1:]:
        factor_of = factor_of * one(*cut)
    return factor_of


def routed_block(key, own, number, rows, amount, top, limit, lean):
    ranking = jax.random.permutation(key, amount)
    crowded, common = shares(amount, rows * top, limit, lean, True), shares(amount, rows * top, limit, lean, False)
    places = jnp.arange(amount)

    def named(sizes, offset_by):
        used = int((sizes > 0).sum())
        fixed = max(1, used // 4)
        passed = fixed + (places - fixed + offset_by * (used - fixed)) % max(1, amount - fixed)
        return jnp.zeros((amount,), jnp.int32).at[ranking[jnp.where(places < fixed, places, passed)]].set(jnp.asarray(sizes, jnp.int32))

    sizes = jnp.where(number % 4 == 0, named(crowded, number // 4), named(common, number - number // 4 - 1))
    mixed = jax.random.permutation(jax.random.fold_in(own, 3), amount)
    donor, receiver = mixed[0:amount // 2 * 2:2], mixed[1:amount // 2 * 2:2]
    slack = jnp.minimum(sizes[donor] - 1, limit - sizes[receiver]) // 2
    slack = jnp.where((donor == ranking[0]) | (receiver == ranking[0]) | (sizes[receiver] == 0), 0, jnp.maximum(slack, 0))
    passed = jax.random.randint(jax.random.fold_in(own, 4), (amount // 2,), 0, 1 << 20) % (slack + 1)
    sizes = sizes.at[donor].add(-passed).at[receiver].add(passed)
    members = jnp.searchsorted(jnp.cumsum(sizes), jnp.arange(rows * top), side="right").astype(jnp.int32)
    listing = members.reshape(top, rows).T
    listing = listing[jax.random.permutation(jax.random.fold_in(own, 1), rows)]
    offset_by = jax.random.randint(jax.random.fold_in(own, 2), (rows, 1), 0, top)
    return jnp.take_along_axis(listing, (jnp.arange(top)[None, :] + offset_by) % top, axis=1)


def shares(count, total, reach, lean, full):
    loads = [(1 << 20) // math.isqrt(standing ** lean) + 1 for standing in range(1, count + 1)]
    largest = reach if full else min(reach, max(-(-total // count), total * loads[0] // sum(loads)))
    least = 1 if total - largest >= count - 1 else 0
    given, rest = [largest] + [least] * (count - 1), total - largest - least * (count - 1)
    while rest > 0:
        movable = [i for i in range(1, count) if given[i] < largest] or [i for i in range(1, count) if given[i] < reach]
        mass, left = sum([loads[i] for i in movable]), rest
        for i in movable:
            extra = min(reach - given[i], max(1, left * loads[i] // mass), rest)
            given[i] = given[i] + extra
            rest = rest - extra
    return np.array(given)


def gaussian(key, extent, scale, reach, shards=(), kind=jnp.bfloat16):
    drawn = jax.random.normal(key, extent, jnp.float32) * scale
    if len(shards) > 0:
        drawn = levels(key, extent, shards, -0.22, 0.18) * drawn
    return jnp.clip(drawn, min=-reach, max=reach).astype(kind)


def setup_inputs(seed: int = 0, part: int = 0) -> dict:
    key_list = jax.random.split(jax.random.key(seed), 7)
    own_keys = jax.random.split(jax.random.fold_in(key_list[6], part), 7)
    tokens = gaussian(own_keys[0], (TOKENS, D), 1.0, 6.0, ((0, 128),))
    cotangent = gaussian(own_keys[1], (TOKENS, D), 1.0, 6.0, ((0, 128),))
    expert_ids_keys = jax.random.split(jax.random.fold_in(own_keys[2], 1), TOKENS // TOK_DEV)
    expert_ids_turns = jax.random.permutation(jax.random.fold_in(own_keys[2], 3), TOKENS // TOK_DEV)
    expert_ids = jax.vmap(lambda own, number: routed_block(jax.random.fold_in(own_keys[2], 2), own, number, TOK_DEV, EXPERTS, TOP, CAP, 2))(expert_ids_keys, expert_ids_turns).reshape((TOKENS, TOP))
    combine = jnp.clip(0.05 + 0.25 * jax.random.uniform(own_keys[3], (TOKENS, TOP), jnp.float32) ** levels(own_keys[3], (TOKENS, TOP), ((0, 128),), -0.2, 0.2), 0.05, 0.3)
    w_gate_up = gaussian(key_list[4], (EXPERTS, D, 2 * FF), D ** -0.5, 0.125, ((0, 128),))
    w_down = gaussian(key_list[5], (EXPERTS, FF, D), FF ** -0.5, 0.3125, ((0, 128),))
    return dict(tokens=tokens, cotangent=cotangent, expert_ids=expert_ids, combine=combine, w_gate_up=w_gate_up, w_down=w_down)


def expert_forward(rows, w_gate_up, w_down):
    width = w_down.shape[0]
    projected = jnp.dot(rows, w_gate_up, preferred_element_type=jnp.float32)
    gate = projected[:, :width]
    upward = projected[:, width:]
    hidden = (gate * jax.nn.sigmoid(gate) * upward).astype(jnp.bfloat16)
    output = jnp.dot(hidden, w_down, preferred_element_type=jnp.float32).astype(jnp.bfloat16)
    return output, gate, upward


def expert_backward(grads, gate, upward, w_gate_up, w_down):
    grad_hidden = lax.dot_general(grads, w_down, (((1,), (1,)), ((), ())), preferred_element_type=jnp.float32)
    sigmoid = jax.nn.sigmoid(gate)
    grad_gate = grad_hidden * upward * sigmoid * (1.0 + gate * (1.0 - sigmoid))
    grad_up = grad_hidden * gate * sigmoid
    paired = jnp.concatenate([grad_gate, grad_up], axis=1).astype(jnp.bfloat16)
    back = lax.dot_general(paired, w_gate_up, (((1,), (1,)), ((), ())), preferred_element_type=jnp.float32)
    return back.astype(jnp.bfloat16)


def reference(tokens, cotangent, expert_ids, combine, w_gate_up, w_down):
    devices = N_NODE * N_LOCAL
    flat_ids = expert_ids.reshape(devices, TOK_DEV * TOP).astype(jnp.int32)
    onehot = (flat_ids[:, :, None] == jnp.arange(EXPERTS, dtype=jnp.int32)[None, None, :]).astype(jnp.int32)
    before = jnp.cumsum(onehot, axis=1).astype(jnp.int32) - onehot
    ranks = jnp.sum(before * onehot, axis=2).astype(jnp.int32)
    source = jnp.arange(devices, dtype=jnp.int32)[:, None]
    slots = (flat_ids * (devices * CAP) + source * CAP + ranks).reshape(-1).astype(jnp.int32)
    total = EXPERTS * devices * CAP
    weights = combine.reshape(-1)
    copies_x = jnp.repeat(tokens, TOP, axis=0)
    copies_g = (jnp.repeat(cotangent.astype(jnp.float32), TOP, axis=0) * weights[:, None]).astype(jnp.bfloat16)
    buffer_x = jnp.zeros((total, D), jnp.bfloat16).at[slots].set(copies_x).reshape(EXPERTS, devices * CAP, D)
    buffer_g = jnp.zeros((total, D), jnp.bfloat16).at[slots].set(copies_g).reshape(EXPERTS, devices * CAP, D)

    def per_expert(items):
        rows, grads, gate_up_one, down_one = items
        output, gate, upward = expert_forward(rows, gate_up_one, down_one)
        back = expert_backward(grads, gate, upward, gate_up_one, down_one)
        return output, back

    outputs, backs = lax.map(per_expert, (buffer_x, buffer_g, w_gate_up, w_down))
    picked = outputs.reshape(total, D)[slots].reshape(TOKENS, TOP, D).astype(jnp.float32)
    picked_back = backs.reshape(total, D)[slots].reshape(TOKENS, TOP, D).astype(jnp.float32)
    mixed = jnp.sum(combine[:, :, None] * picked, axis=1).astype(jnp.bfloat16)
    grad_tokens = jnp.sum(picked_back, axis=1).astype(jnp.bfloat16)
    grad_combine = jnp.sum(picked * cotangent.astype(jnp.float32)[:, None, :], axis=2)
    return mixed, grad_tokens, grad_combine
```

```python
import jax
import jax.numpy as jnp
from jax import lax
from jax.experimental import pallas as pl
from jax.experimental.pallas import tpu as pltpu
from jax.sharding import PartitionSpec as P

EXTRA = 128
F32 = jnp.float32
BF16 = jnp.bfloat16


def split3(value):
    hi = value.astype(BF16)
    rest = value - hi.astype(F32)
    mid = rest.astype(BF16)
    low = (rest - mid.astype(F32)).astype(BF16)
    return hi, mid, low


def dot(a, b):
    return jnp.dot(a, b, preferred_element_type=F32)


def dispatch_kernel(dims, node_ref, all_ref, send_ref, place_ref, hi_ref, mid_ref):
    blocks, rows, peers, cap, top, width = dims
    tokens = blocks * rows
    slots = peers * blocks * cap
    per_peer = blocks * cap
    extra = all_ref[:, 2 * width :].astype(F32)
    base = (node_ref[0] * peers).astype(F32)
    slot = lax.broadcasted_iota(jnp.int32, (tokens, slots), 1)
    wanted = (slot // per_peer).astype(F32) + base
    has = jnp.zeros((tokens, slots), F32)
    weight = jnp.zeros((tokens, slots), F32)
    for k in range(top):
        match = extra[:, k : k + 1] == wanted
        value = (
            extra[:, top + k : top + k + 1]
            + extra[:, 2 * top + k : 2 * top + k + 1]
            + extra[:, 3 * top + k : 3 * top + k + 1]
        )
        has = jnp.where(match, 1.0, has)
        weight = jnp.where(match, value, weight)
    row = lax.broadcasted_iota(jnp.int32, (tokens, tokens), 0)
    col = lax.broadcasted_iota(jnp.int32, (tokens, tokens), 1)
    earlier = jnp.where((row // rows == col // rows) & (col < row), 1.0, 0.0).astype(BF16)
    rank = dot(earlier, has.astype(BF16))
    block = (lax.broadcasted_iota(jnp.int32, (tokens, slots), 0) // rows * cap).astype(F32)
    place = jnp.where((has > 0.0) & (block + rank == (slot % per_peer).astype(F32)), 1.0, 0.0)
    weight = place * weight
    place_bf = place.astype(BF16)
    hi, mid, low = split3(weight)
    place_ref[...] = place_bf
    hi_ref[...] = hi
    mid_ref[...] = mid
    over_tokens = (((0,), (0,)), ((), ()))
    ones = jnp.ones((tokens, 128), BF16)
    slot_weight = (
        lax.dot_general(hi, ones, over_tokens, preferred_element_type=F32)
        + lax.dot_general(mid, ones, over_tokens, preferred_element_type=F32)
        + lax.dot_general(low, ones, over_tokens, preferred_element_type=F32)
    )[:, :1]
    send_ref[:, :width] = lax.dot_general(
        place_bf, all_ref[:, :width], over_tokens, preferred_element_type=F32
    ).astype(BF16)
    picked = lax.dot_general(
        place_bf, all_ref[:, width : 2 * width], over_tokens, preferred_element_type=F32
    )
    send_ref[:, width:] = (picked * slot_weight).astype(BF16)


def expert_kernel(width, rows_ref, gate_up_ref, down_ref, out_ref):
    hidden_width = down_ref.shape[0]
    projected = dot(rows_ref[:, :width], gate_up_ref[...])
    gate = projected[:, :hidden_width]
    upward = projected[:, hidden_width:]
    sigmoid = jax.nn.sigmoid(gate)
    hidden = (gate * sigmoid * upward).astype(BF16)
    out_ref[:, :width] = dot(hidden, down_ref[...]).astype(BF16)
    over_last = (((1,), (1,)), ((), ()))
    grad_hidden = lax.dot_general(
        rows_ref[:, width:], down_ref[...], over_last, preferred_element_type=F32
    )
    grad_gate = grad_hidden * upward * sigmoid * (1.0 + gate * (1.0 - sigmoid))
    grad_up = grad_hidden * gate * sigmoid
    paired = jnp.concatenate([grad_gate.astype(BF16), grad_up.astype(BF16)], axis=1)
    out_ref[:, width:] = lax.dot_general(
        paired, gate_up_ref[...], over_last, preferred_element_type=F32
    ).astype(BF16)


def combine_kernel(dims, node_ref, all_ref, rows_ref, place_ref, hi_ref, mid_ref, sum_ref):
    blocks, rows, peers, cap, top, width = dims
    tokens = blocks * rows
    slots = peers * blocks * cap
    output = rows_ref[:, :width]
    sum_ref[:, :width] = (dot(hi_ref[...], output) + dot(mid_ref[...], output)).astype(BF16)
    sum_ref[:, width : 2 * width] = dot(place_ref[...], rows_ref[:, width:]).astype(BF16)
    over_last = (((1,), (1,)), ((), ()))
    against = lax.dot_general(
        all_ref[:, width : 2 * width], output, over_last, preferred_element_type=F32
    )
    kept = against * place_ref[...].astype(F32)
    peer_of = lax.broadcasted_iota(jnp.int32, (slots, EXTRA), 0) // (blocks * cap)
    lane_of = lax.broadcasted_iota(jnp.int32, (slots, EXTRA), 1)
    fold = jnp.where(peer_of == lane_of, 1.0, 0.0).astype(BF16)
    hi, mid, low = split3(kept)
    by_peer = dot(hi, fold) + dot(mid, fold) + dot(low, fold)
    ids = all_ref[:, 2 * width :].astype(F32)
    base = (node_ref[0] * peers).astype(F32)
    lane = lax.broadcasted_iota(jnp.int32, (tokens, EXTRA), 1)
    chosen = jnp.zeros((tokens, EXTRA), F32)
    for p in range(peers):
        chosen = jnp.where(ids == base + p, by_peer[:, p : p + 1], chosen)
    chosen = jnp.where(lane < top, chosen, 0.0)
    hi, mid, low = split3(chosen)
    sum_ref[:, 2 * width :] = (
        hi.astype(F32)
        + pltpu.roll(mid.astype(F32), top, 1)
        + pltpu.roll(low.astype(F32), 2 * top, 1)
    ).astype(BF16)


def per_device(tokens, cotangent, expert_ids, combine, w_gate_up, w_down):
    blocks = lax.axis_size("node")
    peers = lax.axis_size("local")
    rows, top = expert_ids.shape
    width = tokens.shape[1]
    cap = 2
    dims = (blocks, rows, peers, cap, top, width)
    slots = peers * blocks * cap
    count = blocks * rows
    node = lax.axis_index("node").astype(jnp.int32).reshape(1)
    hi = lax.reduce_precision(combine, 8, 7)
    mid = lax.reduce_precision(combine - hi, 8, 7)
    low = combine - hi - mid
    pieces = (hi.astype(BF16), mid.astype(BF16), low.astype(BF16))
    packed = jnp.concatenate(
        [
            tokens,
            cotangent,
            expert_ids.astype(BF16),
            *pieces,
            jnp.zeros((rows, EXTRA - 4 * top), BF16),
        ],
        axis=1,
    )
    gathered = lax.all_gather(packed, "node", axis=0, tiled=True)
    smem = pl.BlockSpec(memory_space=pltpu.SMEM)
    vmem = pl.BlockSpec(memory_space=pltpu.VMEM)
    send, place, hi, mid = pl.pallas_call(
        lambda *refs: dispatch_kernel(dims, *refs),
        out_shape=(
            jax.ShapeDtypeStruct((slots, 2 * width), BF16),
            jax.ShapeDtypeStruct((count, slots), BF16),
            jax.ShapeDtypeStruct((count, slots), BF16),
            jax.ShapeDtypeStruct((count, slots), BF16),
        ),
        in_specs=[smem, vmem],
        out_specs=(vmem,) * 4,
        name="dispatch",
    )(node, gathered)
    arrived = lax.all_to_all(
        send.reshape(peers, blocks * cap, 2 * width), "local", 0, 0, tiled=True
    )
    worked = pl.pallas_call(
        lambda *refs: expert_kernel(width, *refs),
        out_shape=jax.ShapeDtypeStruct((slots, 2 * width), BF16),
        in_specs=[vmem] * 3,
        out_specs=vmem,
        name="expert",
    )(arrived.reshape(slots, 2 * width), w_gate_up[0], w_down[0])
    returned = lax.all_to_all(
        worked.reshape(peers, blocks * cap, 2 * width), "local", 0, 0, tiled=True
    )
    partial = pl.pallas_call(
        lambda *refs: combine_kernel(dims, *refs),
        out_shape=jax.ShapeDtypeStruct((count, 2 * width + EXTRA), BF16),
        in_specs=[smem] + [vmem] * 5,
        out_specs=vmem,
        name="combine",
    )(node, gathered, returned.reshape(slots, 2 * width), place, hi, mid)
    summed = lax.psum_scatter(partial, "node", scatter_dimension=0, tiled=True)
    last = summed[:, 2 * width :].astype(F32)
    grad_combine = last[:, :top] + last[:, top : 2 * top] + last[:, 2 * top : 3 * top]
    return summed[:, :width], summed[:, width : 2 * width], grad_combine


def solution(mesh):
    rows = P(("dp", "node", "local"), None)
    experts = P(("node", "local"), None, None)
    return jax.shard_map(
        per_device,
        mesh=mesh,
        in_specs=(rows, rows, rows, rows, experts, experts),
        out_specs=(rows, rows, rows),
        check_vma=False,
    )
```

```python
import jax
import jax.numpy as jnp
from jax import lax
from jax.experimental import pallas as pl
from jax.experimental.pallas import tpu as pltpu
from jax.sharding import PartitionSpec as P

EXTRA = 128
QUAD = 4
CAP = 2
STEPS = (0, -4, 4, 8)
F32 = jnp.float32
BF16 = jnp.bfloat16
OVER_FIRST = (((0,), (0,)), ((), ()))
OVER_LAST = (((1,), (1,)), ((), ()))


def split3(value):
    hi = value.astype(BF16)
    rest = value - hi.astype(F32)
    mid = rest.astype(BF16)
    low = (rest - mid.astype(F32)).astype(BF16)
    return hi, mid, low


def dot(a, b):
    return jnp.dot(a, b, preferred_element_type=F32)


def placing(info, node, shift, dims):
    blocks, rows, peers, top = dims
    tokens = QUAD * rows
    per_peer = QUAD * CAP
    slots = QUAD * peers * per_peer
    first = lax.rem(node + blocks - shift, blocks) // QUAD * QUAD + shift
    slot = lax.broadcasted_iota(jnp.int32, (tokens, slots), 1)
    wanted = lax.rem(first * peers + slot // per_peer, blocks * peers).astype(F32)
    ids = info[:, :top]
    weights = info[:, top : 2 * top] + info[:, 2 * top : 3 * top] + info[:, 3 * top : 4 * top]
    has = jnp.zeros((tokens, slots), F32)
    weight = jnp.zeros((tokens, slots), F32)
    for k in range(top):
        match = ids[:, k : k + 1] == wanted
        has = jnp.where(match, 1.0, has)
        weight = jnp.where(match, weights[:, k : k + 1], weight)
    row = lax.broadcasted_iota(jnp.int32, (tokens, tokens), 0)
    col = lax.broadcasted_iota(jnp.int32, (tokens, tokens), 1)
    earlier = jnp.where((row // rows == col // rows) & (col < row), 1.0, 0.0).astype(BF16)
    rank = dot(earlier, has.astype(BF16))
    part = lax.broadcasted_iota(jnp.int32, (tokens, slots), 0) // rows
    offset = jnp.where(part == 0, 0, jnp.where(part == 1, 3, jnp.where(part == 2, 1, 2)))
    block = lax.rem(node // QUAD + offset, QUAD) * CAP
    here = block.astype(F32) + rank == (slot % per_peer).astype(F32)
    place = jnp.where((has > 0.0) & here, 1.0, 0.0)
    return place, place * weight


def gather_rows(refs, lo, hi):
    return jnp.concatenate([ref[:, lo:hi] for ref in refs], axis=0)


def dispatch_x(dims, width, node_ref, a, b, c, d, send_ref, place_ref, hi_ref, mid_ref):
    refs = (a, b, c, d)
    info = gather_rows(refs, 2 * width, 2 * width + EXTRA).astype(F32)
    place, weight = placing(info, node_ref[0], 0, dims)
    place_bf = place.astype(BF16)
    hi, mid, _ = split3(weight)
    place_ref[...] = place_bf
    hi_ref[...] = hi
    mid_ref[...] = mid
    send_ref[...] = lax.dot_general(
        place_bf, gather_rows(refs, 0, width), OVER_FIRST, preferred_element_type=F32
    ).astype(BF16)


def dispatch_g(dims, width, node_ref, a, b, c, d, send_ref, place_ref):
    refs = (a, b, c, d)
    info = gather_rows(refs, 2 * width, 2 * width + EXTRA).astype(F32)
    place, weight = placing(info, node_ref[0], 2, dims)
    place_bf = place.astype(BF16)
    place_ref[...] = place_bf
    ones = jnp.ones((place.shape[0], 128), BF16)
    hi, mid, low = split3(weight)
    slot_weight = (
        lax.dot_general(hi, ones, OVER_FIRST, preferred_element_type=F32)
        + lax.dot_general(mid, ones, OVER_FIRST, preferred_element_type=F32)
        + lax.dot_general(low, ones, OVER_FIRST, preferred_element_type=F32)
    )[:, :1]
    picked = lax.dot_general(
        place_bf, gather_rows(refs, width, 2 * width), OVER_FIRST, preferred_element_type=F32
    )
    send_ref[...] = (picked * slot_weight).astype(BF16)


def expert_forward(rows_ref, gate_up_ref, down_ref, out_ref, gate_ref, up_ref):
    hidden_width = down_ref.shape[0]
    projected = dot(rows_ref[...], gate_up_ref[...])
    gate = projected[:, :hidden_width]
    upward = projected[:, hidden_width:]
    gate_ref[...] = gate
    up_ref[...] = upward
    hidden = (gate * jax.nn.sigmoid(gate) * upward).astype(BF16)
    out_ref[...] = dot(hidden, down_ref[...]).astype(BF16)


def expert_backward(rows_ref, gate_ref, up_ref, gate_up_ref, down_ref, back_ref):
    half = rows_ref.shape[0] // 2
    rows = jnp.concatenate([rows_ref[half:, :], rows_ref[:half, :]], axis=0)
    gate = gate_ref[...]
    upward = up_ref[...]
    sigmoid = jax.nn.sigmoid(gate)
    grad_hidden = lax.dot_general(rows, down_ref[...], OVER_LAST, preferred_element_type=F32)
    grad_gate = grad_hidden * upward * sigmoid * (1.0 + gate * (1.0 - sigmoid))
    grad_up = grad_hidden * gate * sigmoid
    paired = jnp.concatenate([grad_gate.astype(BF16), grad_up.astype(BF16)], axis=1)
    back = lax.dot_general(
        paired, gate_up_ref[...], OVER_LAST, preferred_element_type=F32
    ).astype(BF16)
    back_ref[half:, :] = back[:half]
    back_ref[:half, :] = back[half:]


def combine_out(dims, width, node_ref, a, b, c, d, rows_ref, place_ref, hi_ref, mid_ref, *sums):
    blocks, rows, peers, top = dims
    tokens = QUAD * rows
    per_peer = QUAD * CAP
    slots = QUAD * peers * per_peer
    refs = (a, b, c, d)
    output = rows_ref[...]
    mixed = (dot(hi_ref[...], output) + dot(mid_ref[...], output)).astype(BF16)
    cotangent = gather_rows(refs, width, 2 * width)
    against = lax.dot_general(cotangent, output, OVER_LAST, preferred_element_type=F32)
    kept = against * place_ref[...].astype(F32)
    peer_of = lax.broadcasted_iota(jnp.int32, (slots, EXTRA), 0) // per_peer
    lane_of = lax.broadcasted_iota(jnp.int32, (slots, EXTRA), 1)
    fold = jnp.where(peer_of == lane_of, 1.0, 0.0).astype(BF16)
    hi, mid, low = split3(kept)
    by_peer = dot(hi, fold) + dot(mid, fold) + dot(low, fold)
    ids = gather_rows(refs, 2 * width, 2 * width + EXTRA).astype(F32)
    base = (node_ref[0] // QUAD * (QUAD * peers)).astype(F32)
    lane = lax.broadcasted_iota(jnp.int32, (tokens, EXTRA), 1)
    peer_lane = lane.astype(F32)
    chosen = jnp.zeros((tokens, EXTRA), F32)
    for k in range(top):
        mine = jnp.where(ids[:, k : k + 1] - base == peer_lane, by_peer, 0.0)
        total = jnp.sum(mine, axis=1, keepdims=True)
        chosen = jnp.where(lane == k, total, chosen)
    hi, mid, low = split3(chosen)
    pieces = (
        hi.astype(F32)
        + pltpu.roll(mid.astype(F32), top, 1)
        + pltpu.roll(low.astype(F32), 2 * top, 1)
    ).astype(BF16)
    for i, ref in enumerate(sums):
        ref[:, :width] = mixed[i * rows : (i + 1) * rows]
        ref[:, width:] = pieces[i * rows : (i + 1) * rows]


def combine_back(rows_ref, place_ref, *sums):
    rows = sums[0].shape[0]
    total = dot(place_ref[...], rows_ref[...]).astype(BF16)
    for i, ref in enumerate(sums):
        ref[...] = total[i * rows : (i + 1) * rows]


def final_out(top, width, a, b, c, d, mixed_ref, weights_ref):
    mixed_ref[...] = sum(ref[:, :width].astype(F32) for ref in (a, b, c, d)).astype(BF16)
    last = sum(ref[:, width:].astype(F32) for ref in (a, b, c, d))
    lanes = last.shape[1]
    total = last + pltpu.roll(last, lanes - top, 1) + pltpu.roll(last, lanes - 2 * top, 1)
    weights_ref[...] = total[:, :top]


def final_back(a, b, c, d, grad_ref):
    grad_ref[...] = sum(ref[...].astype(F32) for ref in (a, b, c, d)).astype(BF16)


def per_device(tokens, cotangent, expert_ids, combine, w_gate_up, w_down):
    blocks = lax.axis_size("node")
    peers = lax.axis_size("local")
    rows, top = expert_ids.shape
    width = tokens.shape[1]
    hidden_width = w_down.shape[1]
    dims = (blocks, rows, peers, top)
    count = QUAD * rows
    per_peer = QUAD * CAP
    slots = QUAD * peers * per_peer
    node = lax.axis_index("node").astype(jnp.int32).reshape(1)
    smem = pl.BlockSpec(memory_space=pltpu.SMEM)
    vmem = pl.BlockSpec(memory_space=pltpu.VMEM)

    def shape(*dims, dtype=BF16):
        return jax.ShapeDtypeStruct(dims, dtype)

    def call(name, body, outs, scalars, *operands):
        return pl.pallas_call(
            body,
            out_shape=outs,
            in_specs=[smem] * scalars + [vmem] * (len(operands) - scalars),
            out_specs=(vmem,) * len(outs),
            name=name,
        )(*operands)

    def shifted(value, step):
        pairs = [(i, (i + step) % blocks) for i in range(blocks)]
        return lax.ppermute(value, "node", pairs)

    def quads(shift):
        return [
            [(QUAD * q + shift + j) % blocks * peers + p for j in range(QUAD) for p in range(peers)]
            for q in range(blocks // QUAD)
        ]

    def exchange(value, shift):
        return lax.all_to_all(
            value.reshape(QUAD * peers, per_peer, width),
            ("node", "local"),
            0,
            0,
            axis_index_groups=quads(shift),
            tiled=True,
        ).reshape(slots, width)

    hi = lax.reduce_precision(combine, 8, 7)
    mid = lax.reduce_precision(combine - hi, 8, 7)
    low = combine - hi - mid
    packed = jnp.concatenate(
        [
            tokens,
            cotangent,
            expert_ids.astype(BF16),
            hi.astype(BF16),
            mid.astype(BF16),
            low.astype(BF16),
            jnp.zeros((rows, EXTRA - 4 * top), BF16),
        ],
        axis=1,
    )
    held = (packed, shifted(packed, 4), shifted(packed, -4), shifted(packed, 8))
    place_shape = shape(count, slots)
    send_x, place_x, hi_x, mid_x = call(
        "dispatch_x",
        lambda *refs: dispatch_x(dims, width, *refs),
        (shape(slots, width), place_shape, place_shape, place_shape),
        1,
        node,
        *held,
    )
    x_rows = exchange(send_x, 0)
    send_g, place_g = call(
        "dispatch_g",
        lambda *refs: dispatch_g(dims, width, *refs),
        (shape(slots, width), place_shape),
        1,
        node,
        *held,
    )
    g_rows = exchange(send_g, 2)
    output, gate, upward = call(
        "expert_forward",
        expert_forward,
        (
            shape(slots, width),
            shape(slots, hidden_width, dtype=F32),
            shape(slots, hidden_width, dtype=F32),
        ),
        0,
        x_rows,
        w_gate_up[0],
        w_down[0],
    )
    out_rows = exchange(output, 0)
    (back,) = call(
        "expert_backward",
        expert_backward,
        (shape(slots, width),),
        0,
        g_rows,
        gate,
        upward,
        w_gate_up[0],
        w_down[0],
    )
    back_rows = exchange(back, 2)
    mine = call(
        "combine_out",
        lambda *refs: combine_out(dims, width, *refs),
        (shape(rows, width + EXTRA),) * 4,
        1,
        node,
        *held,
        out_rows,
        place_x,
        hi_x,
        mid_x,
    )
    mine = [mine[0]] + [shifted(value, step) for value, step in zip(mine[1:], STEPS[1:])]
    theirs = call("combine_back", combine_back, (shape(rows, width),) * 4, 0, back_rows, place_g)
    theirs = [theirs[0]] + [shifted(value, step) for value, step in zip(theirs[1:], STEPS[1:])]
    mixed, grad_combine = call(
        "final_out",
        lambda *refs: final_out(top, width, *refs),
        (shape(rows, width), shape(rows, top, dtype=F32)),
        0,
        *mine,
    )
    (grad_tokens,) = call("final_back", final_back, (shape(rows, width),), 0, *theirs)
    return mixed, grad_tokens, grad_combine


def solution(mesh):
    rows = P(("dp", "node", "local"), None)
    experts = P(("node", "local"), None, None)
    return jax.shard_map(
        per_device,
        mesh=mesh,
        in_specs=(rows, rows, rows, rows, experts, experts),
        out_specs=(rows, rows, rows),
        check_vma=False,
    )
```

```python
import jax
import jax.numpy as jnp
from jax import lax
from jax.experimental import pallas as pl
from jax.experimental.pallas import tpu as pltpu
from jax.sharding import PartitionSpec as P

EXTRA = 128
QUAD = 4
CAP = 2
STEPS = (0, -4, 4, 8)
F32 = jnp.float32
BF16 = jnp.bfloat16
OVER_FIRST = (((0,), (0,)), ((), ()))
OVER_LAST = (((1,), (1,)), ((), ()))


def split3(value):
    hi = value.astype(BF16)
    rest = value - hi.astype(F32)
    mid = rest.astype(BF16)
    low = (rest - mid.astype(F32)).astype(BF16)
    return hi, mid, low


def dot(a, b):
    return jnp.dot(a, b, preferred_element_type=F32)


def placing(info, dims, per_peer, slots, first, offset_of):
    blocks, rows, peers, top = dims
    tokens = info.shape[0]
    slot = lax.broadcasted_iota(jnp.int32, (tokens, slots), 1)
    wanted = (first * peers + slot // per_peer).astype(F32)
    ids = info[:, :top]
    weights = info[:, top : 2 * top] + info[:, 2 * top : 3 * top] + info[:, 3 * top : 4 * top]
    has = jnp.zeros((tokens, slots), F32)
    weight = jnp.zeros((tokens, slots), F32)
    for k in range(top):
        match = ids[:, k : k + 1] == wanted
        has = jnp.where(match, 1.0, has)
        weight = jnp.where(match, weights[:, k : k + 1], weight)
    row = lax.broadcasted_iota(jnp.int32, (tokens, tokens), 0)
    col = lax.broadcasted_iota(jnp.int32, (tokens, tokens), 1)
    earlier = jnp.where((row // rows == col // rows) & (col < row), 1.0, 0.0).astype(BF16)
    rank = dot(earlier, has.astype(BF16))
    offset = offset_of(lax.broadcasted_iota(jnp.int32, (tokens, slots), 0) // rows)
    here = offset.astype(F32) + rank == (slot % per_peer).astype(F32)
    place = jnp.where((has > 0.0) & here, 1.0, 0.0)
    return place, place * weight


def gather_rows(refs, lo, hi):
    return jnp.concatenate([ref[:, lo:hi] for ref in refs], axis=0)


def dispatch_x(dims, width, node_ref, a, b, c, d, send_ref, place_ref):
    refs = (a, b, c, d)
    peers = dims[2]
    node = node_ref[0]
    per_peer = QUAD * CAP

    def offset_of(part):
        moved = jnp.where(part == 0, 0, jnp.where(part == 1, 3, jnp.where(part == 2, 1, 2)))
        return lax.rem(node // QUAD + moved, QUAD) * CAP

    info = gather_rows(refs, width, width + EXTRA).astype(F32)
    first = node // QUAD * QUAD
    place, _ = placing(
        info, dims, per_peer, QUAD * peers * per_peer, first, offset_of
    )
    place_bf = place.astype(BF16)
    place_ref[...] = place_bf
    send_ref[...] = lax.dot_general(
        place_bf, gather_rows(refs, 0, width), OVER_FIRST, preferred_element_type=F32
    ).astype(BF16)


def dispatch_g(dims, width, node_ref, all_ref, send_ref, place_ref, hi_ref, mid_ref):
    blocks, rows, peers, top = dims
    per_peer = blocks * CAP

    def offset_of(block):
        return (block % QUAD * QUAD + block // QUAD) * CAP

    info = all_ref[:, width:].astype(F32)
    place, weight = placing(
        info, dims, per_peer, peers * per_peer, node_ref[0], offset_of
    )
    place_bf = place.astype(BF16)
    place_ref[...] = place_bf
    ones = jnp.ones((place.shape[0], 128), BF16)
    hi, mid, low = split3(weight)
    hi_ref[...] = hi
    mid_ref[...] = mid
    slot_weight = (
        lax.dot_general(hi, ones, OVER_FIRST, preferred_element_type=F32)
        + lax.dot_general(mid, ones, OVER_FIRST, preferred_element_type=F32)
        + lax.dot_general(low, ones, OVER_FIRST, preferred_element_type=F32)
    )[:, :1]
    picked = lax.dot_general(
        place_bf, all_ref[:, :width], OVER_FIRST, preferred_element_type=F32
    )
    send_ref[...] = (picked * slot_weight).astype(BF16)


def swap_order(ref, outer, inner):
    group = QUAD * CAP
    return jnp.concatenate(
        [
            ref[(j * inner + i) * group : (j * inner + i + 1) * group, :]
            for i in range(inner)
            for j in range(outer)
        ],
        axis=0,
    )


def expert_forward(peers, rows_ref, gate_up_ref, down_ref, out_ref, gate_ref, up_ref):
    hidden_width = down_ref.shape[0]
    projected = dot(swap_order(rows_ref, QUAD, peers), gate_up_ref[...])
    gate = projected[:, :hidden_width]
    upward = projected[:, hidden_width:]
    gate_ref[...] = gate
    up_ref[...] = upward
    hidden = (gate * jax.nn.sigmoid(gate) * upward).astype(BF16)
    out_ref[...] = dot(hidden, down_ref[...]).astype(BF16)


def expert_backward(peers, rows_ref, gate_ref, up_ref, gate_up_ref, down_ref, back_ref):
    group = QUAD * CAP
    gate = gate_ref[...]
    upward = up_ref[...]
    sigmoid = jax.nn.sigmoid(gate)
    grad_hidden = lax.dot_general(
        rows_ref[...], down_ref[...], OVER_LAST, preferred_element_type=F32
    )
    grad_gate = grad_hidden * upward * sigmoid * (1.0 + gate * (1.0 - sigmoid))
    grad_up = grad_hidden * gate * sigmoid
    paired = jnp.concatenate([grad_gate.astype(BF16), grad_up.astype(BF16)], axis=1)
    back = lax.dot_general(
        paired, gate_up_ref[...], OVER_LAST, preferred_element_type=F32
    ).astype(BF16)
    for p in range(peers):
        for k in range(QUAD):
            here = (p * QUAD + k) * group
            there = (k * peers + p) * group
            back_ref[there : there + group, :] = back[here : here + group]


def combine_out(dims, width, node_ref, all_ref, rows_ref, place_ref, hi_ref, mid_ref, sum_ref):
    blocks, rows, peers, top = dims
    tokens = blocks * rows
    per_peer = blocks * CAP
    slots = peers * per_peer
    output = rows_ref[...]
    sum_ref[:, :width] = (dot(hi_ref[...], output) + dot(mid_ref[...], output)).astype(BF16)
    against = lax.dot_general(
        all_ref[:, :width], output, OVER_LAST, preferred_element_type=F32
    )
    kept = against * place_ref[...].astype(F32)
    peer_of = lax.broadcasted_iota(jnp.int32, (slots, EXTRA), 0) // per_peer
    lane_of = lax.broadcasted_iota(jnp.int32, (slots, EXTRA), 1)
    fold = jnp.where(peer_of == lane_of, 1.0, 0.0).astype(BF16)
    hi, mid, low = split3(kept)
    by_peer = dot(hi, fold) + dot(mid, fold) + dot(low, fold)
    ids = all_ref[:, width:].astype(F32)
    base = (node_ref[0] * peers).astype(F32)
    lane = lax.broadcasted_iota(jnp.int32, (tokens, EXTRA), 1)
    chosen = jnp.zeros((tokens, EXTRA), F32)
    for p in range(peers):
        chosen = jnp.where(ids == base + p, by_peer[:, p : p + 1], chosen)
    chosen = jnp.where(lane < top, chosen, 0.0)
    hi, mid, low = split3(chosen)
    sum_ref[:, width:] = (
        hi.astype(F32)
        + pltpu.roll(mid.astype(F32), top, 1)
        + pltpu.roll(low.astype(F32), 2 * top, 1)
    ).astype(BF16)


def combine_back(rows_ref, place_ref, *sums):
    rows = sums[0].shape[0]
    total = dot(place_ref[...], rows_ref[...]).astype(BF16)
    for i, ref in enumerate(sums):
        ref[...] = total[i * rows : (i + 1) * rows]


def final_out(top, width, all_ref, mixed_ref, weights_ref):
    mixed_ref[...] = all_ref[:, :width]
    last = all_ref[:, width:].astype(F32)
    lanes = last.shape[1]
    total = last + pltpu.roll(last, lanes - top, 1) + pltpu.roll(last, lanes - 2 * top, 1)
    weights_ref[...] = total[:, :top]


def final_back(a, b, c, d, grad_ref):
    grad_ref[...] = sum(ref[...].astype(F32) for ref in (a, b, c, d)).astype(BF16)


def per_device(tokens, cotangent, expert_ids, combine, w_gate_up, w_down):
    blocks = lax.axis_size("node")
    peers = lax.axis_size("local")
    rows, top = expert_ids.shape
    width = tokens.shape[1]
    hidden_width = w_down.shape[1]
    dims = (blocks, rows, peers, top)
    per_peer = QUAD * CAP
    slots = QUAD * peers * per_peer
    node = lax.axis_index("node").astype(jnp.int32).reshape(1)
    smem = pl.BlockSpec(memory_space=pltpu.SMEM)
    vmem = pl.BlockSpec(memory_space=pltpu.VMEM)

    def shape(*dims, dtype=BF16):
        return jax.ShapeDtypeStruct(dims, dtype)

    def call(name, body, outs, scalars, *operands, after=()):
        used = len(operands)

        def kernel(*refs):
            body(*refs[:used], *refs[used + len(after) :])

        return pl.pallas_call(
            kernel,
            out_shape=outs,
            in_specs=[smem] * scalars
            + [vmem] * (used - scalars)
            + [pl.BlockSpec(memory_space=pl.ANY)] * len(after),
            out_specs=(vmem,) * len(outs),
            name=name,
        )(*operands, *after)

    def shifted(value, step):
        pairs = [(i, (i + step) % blocks) for i in range(blocks)]
        return lax.ppermute(value, "node", pairs)

    quads = [
        [(QUAD * q + j) * peers + p for j in range(QUAD) for p in range(peers)]
        for q in range(blocks // QUAD)
    ]

    def exchange_quad(value):
        return lax.all_to_all(
            value.reshape(QUAD * peers, per_peer, width),
            ("node", "local"),
            0,
            0,
            axis_index_groups=quads,
            tiled=True,
        ).reshape(slots, width)

    def exchange_local(value):
        return lax.all_to_all(
            value.reshape(peers, slots // peers, width), "local", 0, 0, tiled=True
        ).reshape(slots, width)

    hi = lax.reduce_precision(combine, 8, 7)
    mid = lax.reduce_precision(combine - hi, 8, 7)
    low = combine - hi - mid
    info = jnp.concatenate(
        [
            expert_ids.astype(BF16),
            hi.astype(BF16),
            mid.astype(BF16),
            low.astype(BF16),
            jnp.zeros((rows, EXTRA - 4 * top), BF16),
        ],
        axis=1,
    )
    packed = jnp.concatenate([tokens, info], axis=1)
    gathered = lax.all_gather(
        jnp.concatenate([cotangent, info], axis=1), "node", axis=0, tiled=True
    )
    held = (packed, shifted(packed, 4), shifted(packed, -4), shifted(packed, 8))
    send_x, place_x = call(
        "dispatch_x",
        lambda *refs: dispatch_x(dims, width, *refs),
        (shape(slots, width), shape(QUAD * rows, slots)),
        1,
        node,
        *held,
    )
    x_rows = exchange_quad(send_x)
    hidden_shape = shape(slots, hidden_width, dtype=F32)
    output, gate, upward = call(
        "expert_forward",
        lambda *refs: expert_forward(peers, *refs),
        (shape(slots, width), hidden_shape, hidden_shape),
        0,
        x_rows,
        w_gate_up[0],
        w_down[0],
    )
    out_rows = exchange_local(output)
    place_shape = shape(blocks * rows, slots)
    send_g, place_g, hi_g, mid_g = call(
        "dispatch_g",
        lambda *refs: dispatch_g(dims, width, *refs),
        (shape(slots, width), place_shape, place_shape, place_shape),
        1,
        node,
        gathered,
        after=(output,),
    )
    g_rows = exchange_local(send_g)
    (back,) = call(
        "expert_backward",
        lambda *refs: expert_backward(peers, *refs),
        (shape(slots, width),),
        0,
        g_rows,
        gate,
        upward,
        w_gate_up[0],
        w_down[0],
    )
    back_rows = exchange_quad(back)
    (partial,) = call(
        "combine_out",
        lambda *refs: combine_out(dims, width, *refs),
        (shape(blocks * rows, width + EXTRA),),
        1,
        node,
        gathered,
        out_rows,
        place_g,
        hi_g,
        mid_g,
    )
    summed = lax.psum_scatter(partial, "node", scatter_dimension=0, tiled=True)
    theirs = call("combine_back", combine_back, (shape(rows, width),) * 4, 0, back_rows, place_x)
    theirs = [theirs[0]] + [shifted(value, step) for value, step in zip(theirs[1:], STEPS[1:])]
    (grad_tokens,) = call("final_back", final_back, (shape(rows, width),), 0, *theirs)
    mixed, grad_combine = call(
        "final_out",
        lambda *refs: final_out(top, width, *refs),
        (shape(rows, width), shape(rows, top, dtype=F32)),
        0,
        summed,
    )
    return mixed, grad_tokens, grad_combine


def solution(mesh):
    rows = P(("dp", "node", "local"), None)
    experts = P(("node", "local"), None, None)
    return jax.shard_map(
        per_device,
        mesh=mesh,
        in_specs=(rows, rows, rows, rows, experts, experts),
        out_specs=(rows, rows, rows),
        check_vma=False,
    )
```

```python
import jax
import jax.numpy as jnp
from jax import lax
from jax.experimental import pallas as pl
from jax.experimental.pallas import tpu as pltpu
from jax.sharding import PartitionSpec as P

EXTRA = 128
QUAD = 4
CAP = 2
F32 = jnp.float32
BF16 = jnp.bfloat16
OVER_FIRST = (((0,), (0,)), ((), ()))
OVER_LAST = (((1,), (1,)), ((), ()))


def split3(value):
    hi = value.astype(BF16)
    rest = value - hi.astype(F32)
    mid = rest.astype(BF16)
    low = (rest - mid.astype(F32)).astype(BF16)
    return hi, mid, low


def dot(a, b):
    return jnp.dot(a, b, preferred_element_type=F32)


def placing(info, dims, per_peer, slots, first, offset_of):
    blocks, rows, peers, top = dims
    tokens = info.shape[0]
    slot = lax.broadcasted_iota(jnp.int32, (tokens, slots), 1)
    wanted = (first * peers + slot // per_peer).astype(F32)
    ids = info[:, :top]
    weights = info[:, top : 2 * top] + info[:, 2 * top : 3 * top] + info[:, 3 * top : 4 * top]
    has = jnp.zeros((tokens, slots), F32)
    weight = jnp.zeros((tokens, slots), F32)
    for k in range(top):
        match = ids[:, k : k + 1] == wanted
        has = jnp.where(match, 1.0, has)
        weight = jnp.where(match, weights[:, k : k + 1], weight)
    row = lax.broadcasted_iota(jnp.int32, (tokens, tokens), 0)
    col = lax.broadcasted_iota(jnp.int32, (tokens, tokens), 1)
    earlier = jnp.where((row // rows == col // rows) & (col < row), 1.0, 0.0).astype(BF16)
    rank = dot(earlier, has.astype(BF16))
    offset = offset_of(lax.broadcasted_iota(jnp.int32, (tokens, slots), 0) // rows)
    here = offset.astype(F32) + rank == (slot % per_peer).astype(F32)
    place = jnp.where((has > 0.0) & here, 1.0, 0.0)
    return place, place * weight


def gather_rows(refs, lo, hi):
    return jnp.concatenate([ref[:, lo:hi] for ref in refs], axis=0)


def dispatch_x(dims, width, node_ref, a, b, c, d, send_ref, place_ref, full_ref, low_ref, mid_ref):
    refs = (a, b, c, d)
    rows, peers = dims[1:3]
    node = node_ref[0]
    per_peer = QUAD * CAP
    for i, ref in enumerate(refs):
        full_ref[i * rows : (i + 1) * rows, :] = ref[:, width:]
        if i < 2:
            low_ref[i * rows : (i + 1) * rows, :] = ref[:, width:]
        if 1 <= i < 3:
            mid_ref[(i - 1) * rows : i * rows, :] = ref[:, width:]

    def offset_of(part):
        return lax.rem(node // QUAD + part + QUAD - 1, QUAD) * CAP

    info = gather_rows(refs, 2 * width, 2 * width + EXTRA).astype(F32)
    first = node // QUAD * QUAD
    place, _ = placing(
        info, dims, per_peer, QUAD * peers * per_peer, first, offset_of
    )
    place_bf = place.astype(BF16)
    place_ref[...] = place_bf
    send_ref[...] = lax.dot_general(
        place_bf, gather_rows(refs, 0, width), OVER_FIRST, preferred_element_type=F32
    ).astype(BF16)


def dispatch_g(dims, width, node_ref, *refs):
    parts, (send_ref, place_ref, hi_ref, mid_ref) = refs[:5], refs[5:]
    blocks, rows, peers, top = dims
    per_peer = blocks * CAP
    node = node_ref[0]

    def offset_of(part):
        group = part // QUAD
        holder = jnp.where(group == 0, 0, jnp.where(group == 1, -1, 1))
        away = jnp.where(group < 3, holder + part % QUAD * QUAD - QUAD, part % QUAD * QUAD - 6)
        source = lax.rem(node + away + blocks, blocks)
        return (source % QUAD * QUAD + source // QUAD) * CAP

    info = gather_rows(parts, width, width + EXTRA).astype(F32)
    place, weight = placing(
        info, dims, per_peer, peers * per_peer, node_ref[0], offset_of
    )
    place_bf = place.astype(BF16)
    place_ref[...] = place_bf
    ones = jnp.ones((place.shape[0], 128), BF16)
    hi, mid, low = split3(weight)
    hi_ref[...] = hi
    mid_ref[...] = mid
    slot_weight = (
        lax.dot_general(hi, ones, OVER_FIRST, preferred_element_type=F32)
        + lax.dot_general(mid, ones, OVER_FIRST, preferred_element_type=F32)
        + lax.dot_general(low, ones, OVER_FIRST, preferred_element_type=F32)
    )[:, :1]
    picked = lax.dot_general(
        place_bf, gather_rows(parts, 0, width), OVER_FIRST, preferred_element_type=F32
    )
    send_ref[...] = (picked * slot_weight).astype(BF16)


def swap_order(ref, outer, inner):
    group = QUAD * CAP
    return jnp.concatenate(
        [
            ref[(j * inner + i) * group : (j * inner + i + 1) * group, :]
            for i in range(inner)
            for j in range(outer)
        ],
        axis=0,
    )


def expert_forward(peers, rows_ref, gate_up_ref, down_ref, out_ref, gate_ref, up_ref):
    hidden_width = down_ref.shape[0]
    projected = dot(swap_order(rows_ref, QUAD, peers), gate_up_ref[...])
    gate = projected[:, :hidden_width]
    upward = projected[:, hidden_width:]
    gate_ref[...] = gate
    up_ref[...] = upward
    hidden = (gate * jax.nn.sigmoid(gate) * upward).astype(BF16)
    out_ref[...] = dot(hidden, down_ref[...]).astype(BF16)


def expert_backward(peers, rows_ref, gate_ref, up_ref, gate_up_ref, down_ref, back_ref):
    group = QUAD * CAP
    gate = gate_ref[...]
    upward = up_ref[...]
    sigmoid = jax.nn.sigmoid(gate)
    grad_hidden = lax.dot_general(
        rows_ref[...], down_ref[...], OVER_LAST, preferred_element_type=F32
    )
    grad_gate = grad_hidden * upward * sigmoid * (1.0 + gate * (1.0 - sigmoid))
    grad_up = grad_hidden * gate * sigmoid
    paired = jnp.concatenate([grad_gate.astype(BF16), grad_up.astype(BF16)], axis=1)
    back = lax.dot_general(
        paired, gate_up_ref[...], OVER_LAST, preferred_element_type=F32
    ).astype(BF16)
    for p in range(peers):
        for k in range(QUAD):
            here = (p * QUAD + k) * group
            there = (k * peers + p) * group
            back_ref[there : there + group, :] = back[here : here + group]


def combine_out(dims, width, node_ref, *refs):
    parts, (rows_ref, place_ref, hi_ref, mid_ref), sums = refs[:5], refs[5:9], refs[9:]
    blocks, rows, peers, top = dims
    tokens = blocks * rows
    per_peer = blocks * CAP
    slots = peers * per_peer
    output = rows_ref[...]
    mixed = (dot(hi_ref[...], output) + dot(mid_ref[...], output)).astype(BF16)
    against = lax.dot_general(
        gather_rows(parts, 0, width), output, OVER_LAST, preferred_element_type=F32
    )
    kept = against * place_ref[...].astype(F32)
    peer_of = lax.broadcasted_iota(jnp.int32, (slots, EXTRA), 0) // per_peer
    lane_of = lax.broadcasted_iota(jnp.int32, (slots, EXTRA), 1)
    fold = jnp.where(peer_of == lane_of, 1.0, 0.0).astype(BF16)
    hi, mid, low = split3(kept)
    by_peer = dot(hi, fold) + dot(mid, fold) + dot(low, fold)
    ids = gather_rows(parts, width, width + EXTRA).astype(F32)
    base = (node_ref[0] * peers).astype(F32)
    lane = lax.broadcasted_iota(jnp.int32, (tokens, EXTRA), 1)
    chosen = jnp.zeros((tokens, EXTRA), F32)
    for p in range(peers):
        chosen = jnp.where(ids == base + p, by_peer[:, p : p + 1], chosen)
    chosen = jnp.where(lane < top, chosen, 0.0)
    hi, mid, low = split3(chosen)
    pieces = (
        hi.astype(F32)
        + pltpu.roll(mid.astype(F32), top, 1)
        + pltpu.roll(low.astype(F32), 2 * top, 1)
    ).astype(BF16)
    start = 0
    for ref in sums:
        stop = start + ref.shape[0]
        ref[:, :width] = mixed[start:stop]
        ref[:, width:] = pieces[start:stop]
        start = stop


def gather_out(own, after, before, low, mid, *sums):
    rows = sums[0].shape[0]
    for i, ref in enumerate(sums):
        here = slice(i * rows, (i + 1) * rows)
        total = own[here, :].astype(F32) + after[here, :].astype(F32) + before[here, :].astype(F32)
        if i < 2:
            total = total + low[here, :].astype(F32)
        if 1 <= i < 3:
            total = total + mid[(i - 1) * rows : i * rows, :].astype(F32)
        ref[...] = total.astype(BF16)


def combine_back(rows_ref, place_ref, *sums):
    rows = sums[0].shape[0]
    total = dot(place_ref[...], rows_ref[...]).astype(BF16)
    for i, ref in enumerate(sums):
        ref[...] = total[i * rows : (i + 1) * rows]


def final_out(top, width, a, b, c, d, mixed_ref, weights_ref):
    mixed_ref[...] = sum(ref[:, :width].astype(F32) for ref in (a, b, c, d)).astype(BF16)
    last = sum(ref[:, width:].astype(F32) for ref in (a, b, c, d))
    lanes = last.shape[1]
    total = last + pltpu.roll(last, lanes - top, 1) + pltpu.roll(last, lanes - 2 * top, 1)
    weights_ref[...] = total[:, :top]


def final_back(a, b, c, d, grad_ref):
    grad_ref[...] = sum(ref[...].astype(F32) for ref in (a, b, c, d)).astype(BF16)


def per_device(tokens, cotangent, expert_ids, combine, w_gate_up, w_down):
    blocks = lax.axis_size("node")
    peers = lax.axis_size("local")
    rows, top = expert_ids.shape
    width = tokens.shape[1]
    hidden_width = w_down.shape[1]
    dims = (blocks, rows, peers, top)
    per_peer = QUAD * CAP
    slots = QUAD * peers * per_peer
    node = lax.axis_index("node").astype(jnp.int32).reshape(1)
    smem = pl.BlockSpec(memory_space=pltpu.SMEM)
    vmem = pl.BlockSpec(memory_space=pltpu.VMEM)

    def shape(*dims, dtype=BF16):
        return jax.ShapeDtypeStruct(dims, dtype)

    def call(name, body, outs, scalars, *operands, after=()):
        used = len(operands)

        def kernel(*refs):
            body(*refs[:used], *refs[used + len(after) :])

        return pl.pallas_call(
            kernel,
            out_shape=outs,
            in_specs=[smem] * scalars
            + [vmem] * (used - scalars)
            + [pl.BlockSpec(memory_space=pl.ANY)] * len(after),
            out_specs=(vmem,) * len(outs),
            name=name,
        )(*operands, *after)

    def shifted(value, step):
        pairs = [(i, (i + step) % blocks) for i in range(blocks)]
        return lax.ppermute(value, "node", pairs)

    quads = [
        [(QUAD * q + j) * peers + p for j in range(QUAD) for p in range(peers)]
        for q in range(blocks // QUAD)
    ]

    def exchange_quad(value):
        return lax.all_to_all(
            value.reshape(QUAD * peers, per_peer, width),
            ("node", "local"),
            0,
            0,
            axis_index_groups=quads,
            tiled=True,
        ).reshape(slots, width)

    def exchange_local(value):
        return lax.all_to_all(
            value.reshape(peers, slots // peers, width), "local", 0, 0, tiled=True
        ).reshape(slots, width)

    hi = lax.reduce_precision(combine, 8, 7)
    mid = lax.reduce_precision(combine - hi, 8, 7)
    low = combine - hi - mid
    info = jnp.concatenate(
        [
            expert_ids.astype(BF16),
            hi.astype(BF16),
            mid.astype(BF16),
            low.astype(BF16),
            jnp.zeros((rows, EXTRA - 4 * top), BF16),
        ],
        axis=1,
    )
    packed = jnp.concatenate([tokens, cotangent, info], axis=1)
    held = (shifted(packed, 4), packed, shifted(packed, -4), shifted(packed, 8))
    wide = width + EXTRA
    send_x, place_x, full, low_half, mid_half = call(
        "dispatch_x",
        lambda *refs: dispatch_x(dims, width, *refs),
        (
            shape(slots, width),
            shape(QUAD * rows, slots),
            shape(QUAD * rows, wide),
            shape(2 * rows, wide),
            shape(2 * rows, wide),
        ),
        1,
        node,
        *held,
    )
    x_rows = exchange_quad(send_x)
    window = (
        full,
        shifted(full, 1),
        shifted(full, -1),
        shifted(low_half, 2),
        shifted(mid_half, -2),
    )
    place_shape = shape(blocks * rows, slots)
    send_g, place_g, hi_g, mid_g = call(
        "dispatch_g",
        lambda *refs: dispatch_g(dims, width, *refs),
        (shape(slots, width), place_shape, place_shape, place_shape),
        1,
        node,
        *window,
    )
    g_rows = exchange_local(send_g)
    hidden_shape = shape(slots, hidden_width, dtype=F32)
    output, gate, upward = call(
        "expert_forward",
        lambda *refs: expert_forward(peers, *refs),
        (shape(slots, width), hidden_shape, hidden_shape),
        0,
        x_rows,
        w_gate_up[0],
        w_down[0],
    )
    out_rows = exchange_local(output)
    (back,) = call(
        "expert_backward",
        lambda *refs: expert_backward(peers, *refs),
        (shape(slots, width),),
        0,
        g_rows,
        gate,
        upward,
        w_gate_up[0],
        w_down[0],
    )
    back_rows = exchange_quad(back)
    sums = call(
        "combine_out",
        lambda *refs: combine_out(dims, width, *refs),
        tuple(shape(part.shape[0], wide) for part in window),
        1,
        node,
        *window,
        out_rows,
        place_g,
        hi_g,
        mid_g,
    )
    mine = call(
        "gather_out",
        gather_out,
        (shape(rows, wide),) * QUAD,
        0,
        sums[0],
        shifted(sums[1], -1),
        shifted(sums[2], 1),
        shifted(sums[3], -2),
        shifted(sums[4], 2),
    )
    mine = (shifted(mine[0], -4), mine[1], shifted(mine[2], 4), shifted(mine[3], 8))
    theirs = call(
        "combine_back", combine_back, (shape(rows, width),) * QUAD, 0, back_rows, place_x
    )
    theirs = (shifted(theirs[0], -4), theirs[1], shifted(theirs[2], 4), shifted(theirs[3], 8))
    mixed, grad_combine = call(
        "final_out",
        lambda *refs: final_out(top, width, *refs),
        (shape(rows, width), shape(rows, top, dtype=F32)),
        0,
        *mine,
    )
    (grad_tokens,) = call("final_back", final_back, (shape(rows, width),), 0, *theirs)
    return mixed, grad_tokens, grad_combine


def solution(mesh):
    rows = P(("dp", "node", "local"), None)
    experts = P(("node", "local"), None, None)
    return jax.shard_map(
        per_device,
        mesh=mesh,
        in_specs=(rows, rows, rows, rows, experts, experts),
        out_specs=(rows, rows, rows),
        check_vma=False,
    )
```

```python
import jax
import jax.numpy as jnp
from jax import lax
from jax.experimental import pallas as pl
from jax.experimental.pallas import tpu as pltpu
from jax.sharding import PartitionSpec as P

EXTRA = 128
PAIR = 2
F32 = jnp.float32
BF16 = jnp.bfloat16


def split3(value):
    hi = value.astype(BF16)
    rest = value - hi.astype(F32)
    mid = rest.astype(BF16)
    low = (rest - mid.astype(F32)).astype(BF16)
    return hi, mid, low


def dot(a, b):
    return jnp.dot(a, b, preferred_element_type=F32)


def dispatch_kernel(dims, node_ref, all_ref, send_ref, place_ref, hi_ref, mid_ref):
    blocks, rows, peers, cap, top, width = dims
    tokens = blocks * rows
    slots = peers * blocks * cap
    per_peer = blocks * cap
    extra = all_ref[:, 2 * width :].astype(F32)
    base = (node_ref[0] * peers).astype(F32)
    slot = lax.broadcasted_iota(jnp.int32, (tokens, slots), 1)
    wanted = (slot // per_peer).astype(F32) + base
    has = jnp.zeros((tokens, slots), F32)
    weight = jnp.zeros((tokens, slots), F32)
    for k in range(top):
        match = extra[:, k : k + 1] == wanted
        value = (
            extra[:, top + k : top + k + 1]
            + extra[:, 2 * top + k : 2 * top + k + 1]
            + extra[:, 3 * top + k : 3 * top + k + 1]
        )
        has = jnp.where(match, 1.0, has)
        weight = jnp.where(match, value, weight)
    row = lax.broadcasted_iota(jnp.int32, (tokens, tokens), 0)
    col = lax.broadcasted_iota(jnp.int32, (tokens, tokens), 1)
    earlier = jnp.where((row // rows == col // rows) & (col < row), 1.0, 0.0).astype(BF16)
    rank = dot(earlier, has.astype(BF16))
    block = (lax.broadcasted_iota(jnp.int32, (tokens, slots), 0) // rows * cap).astype(F32)
    place = jnp.where((has > 0.0) & (block + rank == (slot % per_peer).astype(F32)), 1.0, 0.0)
    weight = place * weight
    place_bf = place.astype(BF16)
    hi, mid, low = split3(weight)
    place_ref[...] = place_bf
    hi_ref[...] = hi
    mid_ref[...] = mid
    over_tokens = (((0,), (0,)), ((), ()))
    ones = jnp.ones((tokens, 128), BF16)
    slot_weight = (
        lax.dot_general(hi, ones, over_tokens, preferred_element_type=F32)
        + lax.dot_general(mid, ones, over_tokens, preferred_element_type=F32)
        + lax.dot_general(low, ones, over_tokens, preferred_element_type=F32)
    )[:, :1]
    send_ref[:, :width] = lax.dot_general(
        place_bf, all_ref[:, :width], over_tokens, preferred_element_type=F32
    ).astype(BF16)
    picked = lax.dot_general(
        place_bf, all_ref[:, width : 2 * width], over_tokens, preferred_element_type=F32
    )
    send_ref[:, width:] = (picked * slot_weight).astype(BF16)


def expert_kernel(width, rows_ref, gate_up_ref, down_ref, out_ref):
    hidden_width = down_ref.shape[0]
    projected = dot(rows_ref[:, :width], gate_up_ref[...])
    gate = projected[:, :hidden_width]
    upward = projected[:, hidden_width:]
    sigmoid = jax.nn.sigmoid(gate)
    hidden = (gate * sigmoid * upward).astype(BF16)
    out_ref[:, :width] = dot(hidden, down_ref[...]).astype(BF16)
    over_last = (((1,), (1,)), ((), ()))
    grad_hidden = lax.dot_general(
        rows_ref[:, width:], down_ref[...], over_last, preferred_element_type=F32
    )
    grad_gate = grad_hidden * upward * sigmoid * (1.0 + gate * (1.0 - sigmoid))
    grad_up = grad_hidden * gate * sigmoid
    paired = jnp.concatenate([grad_gate.astype(BF16), grad_up.astype(BF16)], axis=1)
    out_ref[:, width:] = lax.dot_general(
        paired, gate_up_ref[...], over_last, preferred_element_type=F32
    ).astype(BF16)


def combine_kernel(dims, node_ref, all_ref, rows_ref, place_ref, hi_ref, mid_ref, sum_ref):
    blocks, rows, peers, cap, top, width = dims
    tokens = blocks * rows
    slots = peers * blocks * cap
    output = rows_ref[:, :width]
    sum_ref[:, :width] = (dot(hi_ref[...], output) + dot(mid_ref[...], output)).astype(BF16)
    sum_ref[:, width : 2 * width] = dot(place_ref[...], rows_ref[:, width:]).astype(BF16)
    over_last = (((1,), (1,)), ((), ()))
    against = lax.dot_general(
        all_ref[:, width : 2 * width], output, over_last, preferred_element_type=F32
    )
    kept = against * place_ref[...].astype(F32)
    peer_of = lax.broadcasted_iota(jnp.int32, (slots, EXTRA), 0) // (blocks * cap)
    lane_of = lax.broadcasted_iota(jnp.int32, (slots, EXTRA), 1)
    fold = jnp.where(peer_of == lane_of, 1.0, 0.0).astype(BF16)
    hi, mid, low = split3(kept)
    by_peer = dot(hi, fold) + dot(mid, fold) + dot(low, fold)
    ids = all_ref[:, 2 * width :].astype(F32)
    base = (node_ref[0] * peers).astype(F32)
    lane = lax.broadcasted_iota(jnp.int32, (tokens, EXTRA), 1)
    chosen = jnp.zeros((tokens, EXTRA), F32)
    for p in range(peers):
        chosen = jnp.where(ids == base + p, by_peer[:, p : p + 1], chosen)
    chosen = jnp.where(lane < top, chosen, 0.0)
    hi, mid, low = split3(chosen)
    sum_ref[:, 2 * width :] = (
        hi.astype(F32)
        + pltpu.roll(mid.astype(F32), top, 1)
        + pltpu.roll(low.astype(F32), 2 * top, 1)
    ).astype(BF16)


def per_device(tokens, cotangent, expert_ids, combine, w_gate_up, w_down):
    nodes = lax.axis_size("node")
    locals_ = lax.axis_size("local")
    blocks = nodes // PAIR
    peers = PAIR * locals_
    rings = [list(range(first, nodes, PAIR)) for first in range(PAIR)]
    pairs = [list(range(q * peers, (q + 1) * peers)) for q in range(blocks)]
    rows, top = expert_ids.shape
    width = tokens.shape[1]
    cap = 2
    dims = (blocks, rows, peers, cap, top, width)
    slots = peers * blocks * cap
    count = blocks * rows
    node = (lax.axis_index("node") // PAIR).astype(jnp.int32).reshape(1)
    hi = lax.reduce_precision(combine, 8, 7)
    mid = lax.reduce_precision(combine - hi, 8, 7)
    low = combine - hi - mid
    pieces = (hi.astype(BF16), mid.astype(BF16), low.astype(BF16))
    packed = jnp.concatenate(
        [
            tokens,
            cotangent,
            expert_ids.astype(BF16),
            *pieces,
            jnp.zeros((rows, EXTRA - 4 * top), BF16),
        ],
        axis=1,
    )
    gathered = lax.all_gather(packed, "node", axis_index_groups=rings, axis=0, tiled=True)
    smem = pl.BlockSpec(memory_space=pltpu.SMEM)
    vmem = pl.BlockSpec(memory_space=pltpu.VMEM)
    send, place, hi, mid = pl.pallas_call(
        lambda *refs: dispatch_kernel(dims, *refs),
        out_shape=(
            jax.ShapeDtypeStruct((slots, 2 * width), BF16),
            jax.ShapeDtypeStruct((count, slots), BF16),
            jax.ShapeDtypeStruct((count, slots), BF16),
            jax.ShapeDtypeStruct((count, slots), BF16),
        ),
        in_specs=[smem, vmem],
        out_specs=(vmem,) * 4,
        name="dispatch",
    )(node, gathered)

    def exchange(value):
        return lax.all_to_all(
            value.reshape(peers, blocks * cap, 2 * width),
            ("node", "local"),
            0,
            0,
            axis_index_groups=pairs,
            tiled=True,
        )

    arrived = exchange(send)
    worked = pl.pallas_call(
        lambda *refs: expert_kernel(width, *refs),
        out_shape=jax.ShapeDtypeStruct((slots, 2 * width), BF16),
        in_specs=[vmem] * 3,
        out_specs=vmem,
        name="expert",
    )(arrived.reshape(slots, 2 * width), w_gate_up[0], w_down[0])
    returned = exchange(worked)
    partial = pl.pallas_call(
        lambda *refs: combine_kernel(dims, *refs),
        out_shape=jax.ShapeDtypeStruct((count, 2 * width + EXTRA), BF16),
        in_specs=[smem] + [vmem] * 5,
        out_specs=vmem,
        name="combine",
    )(node, gathered, returned.reshape(slots, 2 * width), place, hi, mid)
    summed = lax.psum_scatter(
        partial, "node", scatter_dimension=0, axis_index_groups=rings, tiled=True
    )
    last = summed[:, 2 * width :].astype(F32)
    grad_combine = last[:, :top] + last[:, top : 2 * top] + last[:, 2 * top : 3 * top]
    return summed[:, :width], summed[:, width : 2 * width], grad_combine


def solution(mesh):
    rows = P(("dp", "node", "local"), None)
    experts = P(("node", "local"), None, None)
    return jax.shard_map(
        per_device,
        mesh=mesh,
        in_specs=(rows, rows, rows, rows, experts, experts),
        out_specs=(rows, rows, rows),
        check_vma=False,
    )
```

```python
import jax
import jax.numpy as jnp
from jax import lax
from jax.experimental import pallas as pl
from jax.experimental.pallas import tpu as pltpu
from jax.sharding import PartitionSpec as P

EXTRA = 128
PAIR = 2
SMALL = 20 << 20
F32 = jnp.float32
BF16 = jnp.bfloat16


def split3(value):
    hi = value.astype(BF16)
    rest = value - hi.astype(F32)
    mid = rest.astype(BF16)
    low = (rest - mid.astype(F32)).astype(BF16)
    return hi, mid, low


def dot(a, b):
    return jnp.dot(a, b, preferred_element_type=F32)


def dispatch_kernel(dims, node_ref, all_ref, send_ref, place_ref, hi_ref, mid_ref):
    blocks, rows, peers, cap, top, width = dims
    tokens = blocks * rows
    slots = peers * blocks * cap
    per_peer = blocks * cap
    extra = all_ref[:, 2 * width :].astype(F32)
    base = (node_ref[0] * peers).astype(F32)
    slot = lax.broadcasted_iota(jnp.int32, (tokens, slots), 1)
    wanted = (slot // per_peer).astype(F32) + base
    has = jnp.zeros((tokens, slots), F32)
    weight = jnp.zeros((tokens, slots), F32)
    for k in range(top):
        match = extra[:, k : k + 1] == wanted
        value = (
            extra[:, top + k : top + k + 1]
            + extra[:, 2 * top + k : 2 * top + k + 1]
            + extra[:, 3 * top + k : 3 * top + k + 1]
        )
        has = jnp.where(match, 1.0, has)
        weight = jnp.where(match, value, weight)
    row = lax.broadcasted_iota(jnp.int32, (tokens, tokens), 0)
    col = lax.broadcasted_iota(jnp.int32, (tokens, tokens), 1)
    earlier = jnp.where((row // rows == col // rows) & (col < row), 1.0, 0.0).astype(BF16)
    rank = dot(earlier, has.astype(BF16))
    block = (lax.broadcasted_iota(jnp.int32, (tokens, slots), 0) // rows * cap).astype(F32)
    place = jnp.where((has > 0.0) & (block + rank == (slot % per_peer).astype(F32)), 1.0, 0.0)
    weight = place * weight
    place_bf = place.astype(BF16)
    hi, mid, low = split3(weight)
    place_ref[...] = place_bf
    hi_ref[...] = hi
    mid_ref[...] = mid
    over_tokens = (((0,), (0,)), ((), ()))
    ones = jnp.ones((tokens, 128), BF16)
    slot_weight = (
        lax.dot_general(hi, ones, over_tokens, preferred_element_type=F32)
        + lax.dot_general(mid, ones, over_tokens, preferred_element_type=F32)
        + lax.dot_general(low, ones, over_tokens, preferred_element_type=F32)
    )[:, :1]
    send_ref[:, :width] = lax.dot_general(
        place_bf, all_ref[:, :width], over_tokens, preferred_element_type=F32
    ).astype(BF16)
    picked = lax.dot_general(
        place_bf, all_ref[:, width : 2 * width], over_tokens, preferred_element_type=F32
    )
    send_ref[:, width:] = (picked * slot_weight).astype(BF16)


def expert_kernel(width, rows_ref, gate_up_ref, down_ref, out_ref):
    hidden_width = down_ref.shape[0]
    projected = dot(rows_ref[:, :width], gate_up_ref[...])
    gate = projected[:, :hidden_width]
    upward = projected[:, hidden_width:]
    sigmoid = jax.nn.sigmoid(gate)
    hidden = (gate * sigmoid * upward).astype(BF16)
    out_ref[:, :width] = dot(hidden, down_ref[...]).astype(BF16)
    over_last = (((1,), (1,)), ((), ()))
    grad_hidden = lax.dot_general(
        rows_ref[:, width:], down_ref[...], over_last, preferred_element_type=F32
    )
    grad_gate = grad_hidden * upward * sigmoid * (1.0 + gate * (1.0 - sigmoid))
    grad_up = grad_hidden * gate * sigmoid
    paired = jnp.concatenate([grad_gate.astype(BF16), grad_up.astype(BF16)], axis=1)
    out_ref[:, width:] = lax.dot_general(
        paired, gate_up_ref[...], over_last, preferred_element_type=F32
    ).astype(BF16)


def combine_kernel(dims, node_ref, all_ref, rows_ref, place_ref, hi_ref, mid_ref, sum_ref):
    blocks, rows, peers, cap, top, width = dims
    tokens = blocks * rows
    slots = peers * blocks * cap
    output = rows_ref[:, :width]
    sum_ref[:, :width] = (dot(hi_ref[...], output) + dot(mid_ref[...], output)).astype(BF16)
    sum_ref[:, width : 2 * width] = dot(place_ref[...], rows_ref[:, width:]).astype(BF16)
    over_last = (((1,), (1,)), ((), ()))
    against = lax.dot_general(
        all_ref[:, width : 2 * width], output, over_last, preferred_element_type=F32
    )
    kept = against * place_ref[...].astype(F32)
    peer_of = lax.broadcasted_iota(jnp.int32, (slots, EXTRA), 0) // (blocks * cap)
    lane_of = lax.broadcasted_iota(jnp.int32, (slots, EXTRA), 1)
    fold = jnp.where(peer_of == lane_of, 1.0, 0.0).astype(BF16)
    hi, mid, low = split3(kept)
    by_peer = dot(hi, fold) + dot(mid, fold) + dot(low, fold)
    ids = all_ref[:, 2 * width :].astype(F32)
    base = (node_ref[0] * peers).astype(F32)
    lane = lax.broadcasted_iota(jnp.int32, (tokens, EXTRA), 1)
    chosen = jnp.zeros((tokens, EXTRA), F32)
    for p in range(peers):
        chosen = jnp.where(ids == base + p, by_peer[:, p : p + 1], chosen)
    chosen = jnp.where(lane < top, chosen, 0.0)
    hi, mid, low = split3(chosen)
    sum_ref[:, 2 * width :] = (
        hi.astype(F32)
        + pltpu.roll(mid.astype(F32), top, 1)
        + pltpu.roll(low.astype(F32), 2 * top, 1)
    ).astype(BF16)


def pack_kernel(tokens_ref, cotangent_ref, ids_ref, combine_ref, out_ref):
    top = ids_ref.shape[0]
    width = tokens_ref.shape[1]
    out_ref[:, :width] = tokens_ref[...]
    out_ref[:, width : 2 * width] = cotangent_ref[...]
    ids = ids_ref[...].astype(F32).astype(BF16)
    row = lax.broadcasted_iota(jnp.int32, (top, EXTRA), 0)
    lane = lax.broadcasted_iota(jnp.int32, (top, EXTRA), 1)
    info = jnp.zeros((out_ref.shape[0], EXTRA), F32)
    for i, piece in enumerate((ids,) + split3(combine_ref[...])):
        spread = jnp.where(lane == row + i * top, 1.0, 0.0).astype(BF16)
        info = info + lax.dot_general(
            piece, spread, (((0,), (0,)), ((), ())), preferred_element_type=F32
        )
    out_ref[:, 2 * width :] = info.astype(BF16)


def unpack_kernel(sum_ref, mixed_ref, grad_ref, weights_ref):
    top = weights_ref.shape[0]
    width = mixed_ref.shape[1]
    mixed_ref[...] = sum_ref[:, :width]
    grad_ref[...] = sum_ref[:, width : 2 * width]
    row = lax.broadcasted_iota(jnp.int32, (top, EXTRA), 0)
    lane = lax.broadcasted_iota(jnp.int32, (top, EXTRA), 1)
    fold = jnp.where((lane % top == row) & (lane < 3 * top), 1.0, 0.0).astype(BF16)
    weights_ref[...] = lax.dot_general(
        fold, sum_ref[:, 2 * width :], (((1,), (1,)), ((), ())), preferred_element_type=F32
    )


def per_device(tokens, cotangent, expert_ids, combine, w_gate_up, w_down):
    nodes = lax.axis_size("node")
    locals_ = lax.axis_size("local")
    blocks = nodes // PAIR
    peers = PAIR * locals_
    rings = [list(range(first, nodes, PAIR)) for first in range(PAIR)]
    pairs = [list(range(q * peers, (q + 1) * peers)) for q in range(blocks)]
    rows, top = expert_ids.shape
    width = tokens.shape[1]
    cap = 2
    dims = (blocks, rows, peers, cap, top, width)
    slots = peers * blocks * cap
    count = blocks * rows
    node = (lax.axis_index("node") // PAIR).astype(jnp.int32).reshape(1)
    smem = pl.BlockSpec(memory_space=pltpu.SMEM)
    vmem = pl.BlockSpec(memory_space=pltpu.VMEM)
    packed = pl.pallas_call(
        pack_kernel,
        out_shape=jax.ShapeDtypeStruct((rows, 2 * width + EXTRA), BF16),
        in_specs=[vmem] * 4,
        out_specs=vmem,
        name="pack",
    )(tokens, cotangent, expert_ids.T, combine.T)
    gathered = lax.all_gather(packed, "node", axis_index_groups=rings, axis=0, tiled=True)
    send, place, hi, mid = pl.pallas_call(
        lambda *refs: dispatch_kernel(dims, *refs),
        out_shape=(
            jax.ShapeDtypeStruct((slots, 2 * width), BF16),
            jax.ShapeDtypeStruct((count, slots), BF16),
            jax.ShapeDtypeStruct((count, slots), BF16),
            jax.ShapeDtypeStruct((count, slots), BF16),
        ),
        in_specs=[smem, vmem],
        out_specs=(vmem,) * 4,
        compiler_params=pltpu.CompilerParams(vmem_limit_bytes=SMALL),
        name="dispatch",
    )(node, gathered)

    def exchange(value):
        return lax.all_to_all(
            value.reshape(peers, blocks * cap, 2 * width),
            ("node", "local"),
            0,
            0,
            axis_index_groups=pairs,
            tiled=True,
        )

    arrived = exchange(send)
    worked = pl.pallas_call(
        lambda *refs: expert_kernel(width, *refs),
        out_shape=jax.ShapeDtypeStruct((slots, 2 * width), BF16),
        in_specs=[vmem] * 3,
        out_specs=vmem,
        compiler_params=pltpu.CompilerParams(vmem_limit_bytes=SMALL),
        name="expert",
    )(arrived.reshape(slots, 2 * width), w_gate_up[0], w_down[0])
    returned = exchange(worked)
    partial = pl.pallas_call(
        lambda *refs: combine_kernel(dims, *refs),
        out_shape=jax.ShapeDtypeStruct((count, 2 * width + EXTRA), BF16),
        in_specs=[smem] + [vmem] * 5,
        out_specs=vmem,
        compiler_params=pltpu.CompilerParams(vmem_limit_bytes=SMALL),
        name="combine",
    )(node, gathered, returned.reshape(slots, 2 * width), place, hi, mid)
    summed = lax.psum_scatter(
        partial, "node", scatter_dimension=0, axis_index_groups=rings, tiled=True
    )
    mixed, grad_tokens, grad_combine = pl.pallas_call(
        unpack_kernel,
        out_shape=(
            jax.ShapeDtypeStruct((rows, width), BF16),
            jax.ShapeDtypeStruct((rows, width), BF16),
            jax.ShapeDtypeStruct((top, rows), F32),
        ),
        in_specs=[vmem],
        out_specs=(vmem,) * 3,
        name="unpack",
    )(summed)
    return mixed, grad_tokens, grad_combine.T


def solution(mesh):
    rows = P(("dp", "node", "local"), None)
    experts = P(("node", "local"), None, None)
    return jax.shard_map(
        per_device,
        mesh=mesh,
        in_specs=(rows, rows, rows, rows, experts, experts),
        out_specs=(rows, rows, rows),
        check_vma=False,
    )
```

```python
import jax
import jax.numpy as jnp
from jax import lax
from jax.experimental import pallas as pl
from jax.experimental.pallas import tpu as pltpu
from jax.sharding import PartitionSpec as P

EXTRA = 128
PAIR = 4
SMALL = 20 << 20
F32 = jnp.float32
BF16 = jnp.bfloat16


def split3(value):
    hi = value.astype(BF16)
    rest = value - hi.astype(F32)
    mid = rest.astype(BF16)
    low = (rest - mid.astype(F32)).astype(BF16)
    return hi, mid, low


def dot(a, b):
    return jnp.dot(a, b, preferred_element_type=F32)


def dispatch_kernel(dims, node_ref, all_ref, send_ref, place_ref, hi_ref, mid_ref):
    blocks, rows, peers, cap, top, width = dims
    tokens = blocks * rows
    slots = peers * blocks * cap
    per_peer = blocks * cap
    extra = all_ref[:, 2 * width :].astype(F32)
    base = (node_ref[0] * peers).astype(F32)
    slot = lax.broadcasted_iota(jnp.int32, (tokens, slots), 1)
    wanted = (slot // per_peer).astype(F32) + base
    has = jnp.zeros((tokens, slots), F32)
    weight = jnp.zeros((tokens, slots), F32)
    for k in range(top):
        match = extra[:, k : k + 1] == wanted
        value = (
            extra[:, top + k : top + k + 1]
            + extra[:, 2 * top + k : 2 * top + k + 1]
            + extra[:, 3 * top + k : 3 * top + k + 1]
        )
        has = jnp.where(match, 1.0, has)
        weight = jnp.where(match, value, weight)
    row = lax.broadcasted_iota(jnp.int32, (tokens, tokens), 0)
    col = lax.broadcasted_iota(jnp.int32, (tokens, tokens), 1)
    earlier = jnp.where((row // rows == col // rows) & (col < row), 1.0, 0.0).astype(BF16)
    rank = dot(earlier, has.astype(BF16))
    block = (lax.broadcasted_iota(jnp.int32, (tokens, slots), 0) // rows * cap).astype(F32)
    place = jnp.where((has > 0.0) & (block + rank == (slot % per_peer).astype(F32)), 1.0, 0.0)
    weight = place * weight
    place_bf = place.astype(BF16)
    hi, mid, low = split3(weight)
    place_ref[...] = place_bf
    hi_ref[...] = hi
    mid_ref[...] = mid
    over_tokens = (((0,), (0,)), ((), ()))
    ones = jnp.ones((tokens, 128), BF16)
    slot_weight = (
        lax.dot_general(hi, ones, over_tokens, preferred_element_type=F32)
        + lax.dot_general(mid, ones, over_tokens, preferred_element_type=F32)
        + lax.dot_general(low, ones, over_tokens, preferred_element_type=F32)
    )[:, :1]
    send_ref[:, :width] = lax.dot_general(
        place_bf, all_ref[:, :width], over_tokens, preferred_element_type=F32
    ).astype(BF16)
    picked = lax.dot_general(
        place_bf, all_ref[:, width : 2 * width], over_tokens, preferred_element_type=F32
    )
    send_ref[:, width:] = (picked * slot_weight).astype(BF16)


def expert_kernel(width, rows_ref, gate_up_ref, down_ref, out_ref):
    hidden_width = down_ref.shape[0]
    projected = dot(rows_ref[:, :width], gate_up_ref[...])
    gate = projected[:, :hidden_width]
    upward = projected[:, hidden_width:]
    sigmoid = jax.nn.sigmoid(gate)
    hidden = (gate * sigmoid * upward).astype(BF16)
    out_ref[:, :width] = dot(hidden, down_ref[...]).astype(BF16)
    over_last = (((1,), (1,)), ((), ()))
    grad_hidden = lax.dot_general(
        rows_ref[:, width:], down_ref[...], over_last, preferred_element_type=F32
    )
    grad_gate = grad_hidden * upward * sigmoid * (1.0 + gate * (1.0 - sigmoid))
    grad_up = grad_hidden * gate * sigmoid
    paired = jnp.concatenate([grad_gate.astype(BF16), grad_up.astype(BF16)], axis=1)
    out_ref[:, width:] = lax.dot_general(
        paired, gate_up_ref[...], over_last, preferred_element_type=F32
    ).astype(BF16)


def combine_kernel(
    dims, node_ref, all_ref, rows_ref, place_ref, hi_ref, mid_ref, *rest
):
    sums, sum_ref = rest[:-1], rest[-1]
    blocks, rows, peers, cap, top, width = dims
    tokens = blocks * rows
    slots = peers * blocks * cap
    output = rows_ref[:, :width]
    sum_ref[:, :width] = dot(hi_ref[...], output) + dot(mid_ref[...], output)
    sum_ref[:, width : 2 * width] = dot(place_ref[...], rows_ref[:, width:])
    over_last = (((1,), (1,)), ((), ()))
    against = lax.dot_general(
        all_ref[:, width : 2 * width], output, over_last, preferred_element_type=F32
    )
    kept = against * place_ref[...].astype(F32)
    peer_of = lax.broadcasted_iota(jnp.int32, (slots, EXTRA), 0) // (blocks * cap)
    lane_of = lax.broadcasted_iota(jnp.int32, (slots, EXTRA), 1)
    fold = jnp.where(peer_of == lane_of, 1.0, 0.0).astype(BF16)
    hi, mid, low = split3(kept)
    by_peer = dot(hi, fold) + dot(mid, fold) + dot(low, fold)
    ids = all_ref[:, 2 * width :].astype(F32)
    base = (node_ref[0] * peers).astype(F32)
    lane = lax.broadcasted_iota(jnp.int32, (tokens, EXTRA), 1)
    chosen = jnp.zeros((tokens, EXTRA), F32)
    for p in range(peers):
        chosen = jnp.where(ids == base + p, by_peer[:, p : p + 1], chosen)
    chosen = jnp.where(lane < top, chosen, 0.0)
    hi, mid, low = split3(chosen)
    sum_ref[:, 2 * width :] = (
        hi.astype(F32)
        + pltpu.roll(mid.astype(F32), top, 1)
        + pltpu.roll(low.astype(F32), 2 * top, 1)
    )
    for step, ref in enumerate(sums):
        block = lax.rem(node_ref[0] + step, blocks)
        ref[...] = sum_ref[pl.ds(pl.multiple_of(block * rows, rows), rows), :].astype(BF16)


def pack_kernel(tokens_ref, cotangent_ref, ids_ref, combine_ref, out_ref):
    top = ids_ref.shape[0]
    width = tokens_ref.shape[1]
    out_ref[:, :width] = tokens_ref[...]
    out_ref[:, width : 2 * width] = cotangent_ref[...]
    ids = ids_ref[...].astype(F32).astype(BF16)
    row = lax.broadcasted_iota(jnp.int32, (top, EXTRA), 0)
    lane = lax.broadcasted_iota(jnp.int32, (top, EXTRA), 1)
    info = jnp.zeros((out_ref.shape[0], EXTRA), F32)
    for i, piece in enumerate((ids,) + split3(combine_ref[...])):
        spread = jnp.where(lane == row + i * top, 1.0, 0.0).astype(BF16)
        info = info + lax.dot_general(
            piece, spread, (((0,), (0,)), ((), ())), preferred_element_type=F32
        )
    out_ref[:, 2 * width :] = info.astype(BF16)


def unpack_kernel(*refs):
    parts, (mixed_ref, grad_ref, weights_ref) = refs[:-3], refs[-3:]
    top = weights_ref.shape[0]
    width = mixed_ref.shape[1]
    mixed_ref[...] = sum(ref[:, :width].astype(F32) for ref in parts).astype(BF16)
    grad_ref[...] = sum(ref[:, width : 2 * width].astype(F32) for ref in parts).astype(BF16)
    row = lax.broadcasted_iota(jnp.int32, (top, EXTRA), 0)
    lane = lax.broadcasted_iota(jnp.int32, (top, EXTRA), 1)
    fold = jnp.where((lane % top == row) & (lane < 3 * top), 1.0, 0.0).astype(BF16)
    weights_ref[...] = sum(
        lax.dot_general(
            fold, ref[:, 2 * width :], (((1,), (1,)), ((), ())), preferred_element_type=F32
        )
        for ref in parts
    )


def per_device(tokens, cotangent, expert_ids, combine, w_gate_up, w_down):
    nodes = lax.axis_size("node")
    locals_ = lax.axis_size("local")
    blocks = nodes // PAIR
    peers = PAIR * locals_
    rings = [list(range(first, nodes, PAIR)) for first in range(PAIR)]
    pairs = [list(range(q * peers, (q + 1) * peers)) for q in range(blocks)]
    rows, top = expert_ids.shape
    width = tokens.shape[1]
    cap = 2
    dims = (blocks, rows, peers, cap, top, width)
    slots = peers * blocks * cap
    count = blocks * rows
    node = (lax.axis_index("node") // PAIR).astype(jnp.int32).reshape(1)
    smem = pl.BlockSpec(memory_space=pltpu.SMEM)
    vmem = pl.BlockSpec(memory_space=pltpu.VMEM)
    packed = pl.pallas_call(
        pack_kernel,
        out_shape=jax.ShapeDtypeStruct((rows, 2 * width + EXTRA), BF16),
        in_specs=[vmem] * 4,
        out_specs=vmem,
        name="pack",
    )(tokens, cotangent, expert_ids.T, combine.T)
    gathered = lax.all_gather(packed, "node", axis_index_groups=rings, axis=0, tiled=True)
    send, place, hi, mid = pl.pallas_call(
        lambda *refs: dispatch_kernel(dims, *refs),
        out_shape=(
            jax.ShapeDtypeStruct((slots, 2 * width), BF16),
            jax.ShapeDtypeStruct((count, slots), BF16),
            jax.ShapeDtypeStruct((count, slots), BF16),
            jax.ShapeDtypeStruct((count, slots), BF16),
        ),
        in_specs=[smem, vmem],
        out_specs=(vmem,) * 4,
        compiler_params=pltpu.CompilerParams(vmem_limit_bytes=SMALL),
        name="dispatch",
    )(node, gathered)

    def exchange(value):
        return lax.all_to_all(
            value.reshape(peers, blocks * cap, 2 * width),
            ("node", "local"),
            0,
            0,
            axis_index_groups=pairs,
            tiled=True,
        )

    arrived = exchange(send)
    worked = pl.pallas_call(
        lambda *refs: expert_kernel(width, *refs),
        out_shape=jax.ShapeDtypeStruct((slots, 2 * width), BF16),
        in_specs=[vmem] * 3,
        out_specs=vmem,
        compiler_params=pltpu.CompilerParams(vmem_limit_bytes=SMALL),
        name="expert",
    )(arrived.reshape(slots, 2 * width), w_gate_up[0], w_down[0])
    returned = exchange(worked)
    block = jax.ShapeDtypeStruct((rows, 2 * width + EXTRA), BF16)
    partial = pl.pallas_call(
        lambda *refs: combine_kernel(dims, *refs),
        out_shape=(block,) * blocks,
        in_specs=[smem] + [vmem] * 5,
        out_specs=(vmem,) * blocks,
        scratch_shapes=[pltpu.VMEM((count, 2 * width + EXTRA), F32)],
        compiler_params=pltpu.CompilerParams(vmem_limit_bytes=SMALL),
        name="combine",
    )(node, gathered, returned.reshape(slots, 2 * width), place, hi, mid)
    parts = [partial[0]]
    for step in range(1, blocks):
        moves = [(i, (i + step * PAIR) % nodes) for i in range(nodes)]
        parts.append(lax.ppermute(partial[step], "node", moves))
    mixed, grad_tokens, grad_combine = pl.pallas_call(
        unpack_kernel,
        out_shape=(
            jax.ShapeDtypeStruct((rows, width), BF16),
            jax.ShapeDtypeStruct((rows, width), BF16),
            jax.ShapeDtypeStruct((top, rows), F32),
        ),
        in_specs=[vmem] * blocks,
        out_specs=(vmem,) * 3,
        name="unpack",
    )(*parts)
    return mixed, grad_tokens, grad_combine.T


def solution(mesh):
    rows = P(("dp", "node", "local"), None)
    experts = P(("node", "local"), None, None)
    return jax.shard_map(
        per_device,
        mesh=mesh,
        in_specs=(rows, rows, rows, rows, experts, experts),
        out_specs=(rows, rows, rows),
        check_vma=False,
    )
```

```python
import jax
import jax.numpy as jnp
from jax import lax
from jax.experimental import pallas as pl
from jax.experimental.pallas import tpu as pltpu
from jax.sharding import PartitionSpec as P

EXTRA = 128
PAIR = 4
SMALL = 20 << 20
F32 = jnp.float32
BF16 = jnp.bfloat16


def split3(value):
    hi = value.astype(BF16)
    rest = value - hi.astype(F32)
    mid = rest.astype(BF16)
    low = (rest - mid.astype(F32)).astype(BF16)
    return hi, mid, low


def dot(a, b):
    return jnp.dot(a, b, preferred_element_type=F32)


def dispatch_kernel(dims, node_ref, all_ref, send_ref, place_ref, hi_ref, mid_ref):
    blocks, rows, peers, cap, top, width = dims
    tokens = blocks * rows
    slots = peers * blocks * cap
    per_peer = blocks * cap
    extra = all_ref[:, 2 * width :].astype(F32)
    base = (node_ref[0] * peers).astype(F32)
    slot = lax.broadcasted_iota(jnp.int32, (tokens, slots), 1)
    wanted = (slot // per_peer).astype(F32) + base
    has = jnp.zeros((tokens, slots), F32)
    weight = jnp.zeros((tokens, slots), F32)
    for k in range(top):
        match = extra[:, k : k + 1] == wanted
        value = (
            extra[:, top + k : top + k + 1]
            + extra[:, 2 * top + k : 2 * top + k + 1]
            + extra[:, 3 * top + k : 3 * top + k + 1]
        )
        has = jnp.where(match, 1.0, has)
        weight = jnp.where(match, value, weight)
    row = lax.broadcasted_iota(jnp.int32, (tokens, tokens), 0)
    col = lax.broadcasted_iota(jnp.int32, (tokens, tokens), 1)
    earlier = jnp.where((row // rows == col // rows) & (col < row), 1.0, 0.0).astype(BF16)
    rank = dot(earlier, has.astype(BF16))
    block = (lax.broadcasted_iota(jnp.int32, (tokens, slots), 0) // rows * cap).astype(F32)
    place = jnp.where((has > 0.0) & (block + rank == (slot % per_peer).astype(F32)), 1.0, 0.0)
    weight = place * weight
    place_bf = place.astype(BF16)
    hi, mid, low = split3(weight)
    place_ref[...] = place_bf
    hi_ref[...] = hi
    mid_ref[...] = mid
    over_tokens = (((0,), (0,)), ((), ()))
    ones = jnp.ones((tokens, 128), BF16)
    slot_weight = (
        lax.dot_general(hi, ones, over_tokens, preferred_element_type=F32)
        + lax.dot_general(mid, ones, over_tokens, preferred_element_type=F32)
        + lax.dot_general(low, ones, over_tokens, preferred_element_type=F32)
    )[:, :1]
    send_ref[:, :width] = lax.dot_general(
        place_bf, all_ref[:, :width], over_tokens, preferred_element_type=F32
    ).astype(BF16)
    picked = lax.dot_general(
        place_bf, all_ref[:, width : 2 * width], over_tokens, preferred_element_type=F32
    )
    send_ref[:, width:] = (picked * slot_weight).astype(BF16)


def expert_kernel(width, rows_ref, gate_up_ref, down_ref, out_ref):
    hidden_width = down_ref.shape[0]
    projected = dot(rows_ref[:, :width], gate_up_ref[...])
    gate = projected[:, :hidden_width]
    upward = projected[:, hidden_width:]
    sigmoid = jax.nn.sigmoid(gate)
    hidden = (gate * sigmoid * upward).astype(BF16)
    out_ref[:, :width] = dot(hidden, down_ref[...]).astype(BF16)
    over_last = (((1,), (1,)), ((), ()))
    grad_hidden = lax.dot_general(
        rows_ref[:, width:], down_ref[...], over_last, preferred_element_type=F32
    )
    grad_gate = grad_hidden * upward * sigmoid * (1.0 + gate * (1.0 - sigmoid))
    grad_up = grad_hidden * gate * sigmoid
    paired = jnp.concatenate([grad_gate.astype(BF16), grad_up.astype(BF16)], axis=1)
    out_ref[:, width:] = lax.dot_general(
        paired, gate_up_ref[...], over_last, preferred_element_type=F32
    ).astype(BF16)


def combine_kernel(
    dims, node_ref, all_ref, rows_ref, place_ref, hi_ref, mid_ref, *rest
):
    sums, sum_ref = rest[:-1], rest[-1]
    blocks, rows, peers, cap, top, width = dims
    tokens = blocks * rows
    slots = peers * blocks * cap
    output = rows_ref[:, :width]
    sum_ref[:, :width] = dot(hi_ref[...], output) + dot(mid_ref[...], output)
    sum_ref[:, width : 2 * width] = dot(place_ref[...], rows_ref[:, width:])
    over_last = (((1,), (1,)), ((), ()))
    against = lax.dot_general(
        all_ref[:, width : 2 * width], output, over_last, preferred_element_type=F32
    )
    kept = against * place_ref[...].astype(F32)
    peer_of = lax.broadcasted_iota(jnp.int32, (slots, EXTRA), 0) // (blocks * cap)
    lane_of = lax.broadcasted_iota(jnp.int32, (slots, EXTRA), 1)
    fold = jnp.where(peer_of == lane_of, 1.0, 0.0).astype(BF16)
    hi, mid, low = split3(kept)
    by_peer = dot(hi, fold) + dot(mid, fold) + dot(low, fold)
    ids = all_ref[:, 2 * width :].astype(F32)
    base = (node_ref[0] * peers).astype(F32)
    lane = lax.broadcasted_iota(jnp.int32, (tokens, EXTRA), 1)
    chosen = jnp.zeros((tokens, EXTRA), F32)
    for p in range(peers):
        chosen = jnp.where(ids == base + p, by_peer[:, p : p + 1], chosen)
    chosen = jnp.where(lane < top, chosen, 0.0)
    hi, mid, low = split3(chosen)
    sum_ref[:, 2 * width :] = (
        hi.astype(F32)
        + pltpu.roll(mid.astype(F32), top, 1)
        + pltpu.roll(low.astype(F32), 2 * top, 1)
    )
    for step, ref in enumerate(sums):
        block = lax.rem(node_ref[0] + step, blocks)
        ref[...] = sum_ref[pl.ds(pl.multiple_of(block * rows, rows), rows), :].astype(BF16)


def pack_kernel(tokens_ref, cotangent_ref, ids_ref, combine_ref, out_ref):
    top = ids_ref.shape[0]
    width = tokens_ref.shape[1]
    out_ref[:, :width] = tokens_ref[...]
    out_ref[:, width : 2 * width] = cotangent_ref[...]
    ids = ids_ref[...].astype(F32).astype(BF16)
    row = lax.broadcasted_iota(jnp.int32, (top, EXTRA), 0)
    lane = lax.broadcasted_iota(jnp.int32, (top, EXTRA), 1)
    info = jnp.zeros((out_ref.shape[0], EXTRA), F32)
    for i, piece in enumerate((ids,) + split3(combine_ref[...])):
        spread = jnp.where(lane == row + i * top, 1.0, 0.0).astype(BF16)
        info = info + lax.dot_general(
            piece, spread, (((0,), (0,)), ((), ())), preferred_element_type=F32
        )
    out_ref[:, 2 * width :] = info.astype(BF16)


def unpack_kernel(*refs):
    parts, (mixed_ref, grad_ref, weights_ref) = refs[:-3], refs[-3:]
    top = weights_ref.shape[0]
    width = mixed_ref.shape[1]
    mixed_ref[...] = sum(ref[:, :width].astype(F32) for ref in parts).astype(BF16)
    grad_ref[...] = sum(ref[:, width : 2 * width].astype(F32) for ref in parts).astype(BF16)
    row = lax.broadcasted_iota(jnp.int32, (top, EXTRA), 0)
    lane = lax.broadcasted_iota(jnp.int32, (top, EXTRA), 1)
    fold = jnp.where((lane % top == row) & (lane < 3 * top), 1.0, 0.0).astype(BF16)
    weights_ref[...] = sum(
        lax.dot_general(
            fold, ref[:, 2 * width :], (((1,), (1,)), ((), ())), preferred_element_type=F32
        )
        for ref in parts
    )


def per_device(tokens, cotangent, expert_ids, combine, w_gate_up, w_down):
    nodes = lax.axis_size("node")
    locals_ = lax.axis_size("local")
    blocks = nodes // PAIR
    peers = PAIR * locals_
    rings = [list(range(first, nodes, PAIR)) for first in range(PAIR)]
    pairs = [list(range(q * peers, (q + 1) * peers)) for q in range(blocks)]
    rows, top = expert_ids.shape
    width = tokens.shape[1]
    cap = 2
    dims = (blocks, rows, peers, cap, top, width)
    slots = peers * blocks * cap
    count = blocks * rows
    node = (lax.axis_index("node") // PAIR).astype(jnp.int32).reshape(1)
    smem = pl.BlockSpec(memory_space=pltpu.SMEM)
    vmem = pl.BlockSpec(memory_space=pltpu.VMEM)
    packed = pl.pallas_call(
        pack_kernel,
        out_shape=jax.ShapeDtypeStruct((rows, 2 * width + EXTRA), BF16),
        in_specs=[vmem] * 4,
        out_specs=vmem,
        name="pack",
    )(tokens, cotangent, expert_ids.T, combine.T)
    gathered = lax.all_gather(packed, "node", axis_index_groups=rings, axis=0, tiled=True)
    send, place, hi, mid = pl.pallas_call(
        lambda *refs: dispatch_kernel(dims, *refs),
        out_shape=(
            jax.ShapeDtypeStruct((slots, 2 * width), BF16),
            jax.ShapeDtypeStruct((count, slots), BF16),
            jax.ShapeDtypeStruct((count, slots), BF16),
            jax.ShapeDtypeStruct((count, slots), BF16),
        ),
        in_specs=[smem, vmem],
        out_specs=(vmem,) * 4,
        compiler_params=pltpu.CompilerParams(vmem_limit_bytes=SMALL),
        name="dispatch",
    )(node, gathered)

    def exchange(value):
        return lax.all_to_all(
            value.reshape(peers, blocks * cap, 2 * width),
            ("node", "local"),
            0,
            0,
            axis_index_groups=pairs,
            tiled=True,
        )

    arrived = exchange(send)
    worked = pl.pallas_call(
        lambda *refs: expert_kernel(width, *refs),
        out_shape=jax.ShapeDtypeStruct((slots, 2 * width), BF16),
        in_specs=[vmem] * 3,
        out_specs=vmem,
        compiler_params=pltpu.CompilerParams(vmem_limit_bytes=SMALL),
        name="expert",
    )(arrived.reshape(slots, 2 * width), w_gate_up[0], w_down[0])
    returned = exchange(worked)
    block = jax.ShapeDtypeStruct((rows, 2 * width + EXTRA), BF16)
    partial = pl.pallas_call(
        lambda *refs: combine_kernel(dims, *refs),
        out_shape=(block,) * blocks,
        in_specs=[smem] + [vmem] * 5,
        out_specs=(vmem,) * blocks,
        scratch_shapes=[pltpu.VMEM((count, 2 * width + EXTRA), F32)],
        compiler_params=pltpu.CompilerParams(vmem_limit_bytes=SMALL),
        name="combine",
    )(node, gathered, returned.reshape(slots, 2 * width), place, hi, mid)
    parts = [partial[0]]
    for step in [1, blocks - 1, *range(2, blocks - 1)]:
        moves = [(i, (i + step * PAIR) % nodes) for i in range(nodes)]
        parts.append(lax.ppermute(partial[step], "node", moves))
    mixed, grad_tokens, grad_combine = pl.pallas_call(
        unpack_kernel,
        out_shape=(
            jax.ShapeDtypeStruct((rows, width), BF16),
            jax.ShapeDtypeStruct((rows, width), BF16),
            jax.ShapeDtypeStruct((top, rows), F32),
        ),
        in_specs=[vmem] * blocks,
        out_specs=(vmem,) * 3,
        name="unpack",
    )(*parts)
    return mixed, grad_tokens, grad_combine.T


def solution(mesh):
    rows = P(("dp", "node", "local"), None)
    experts = P(("node", "local"), None, None)
    return jax.shard_map(
        per_device,
        mesh=mesh,
        in_specs=(rows, rows, rows, rows, experts, experts),
        out_specs=(rows, rows, rows),
        check_vma=False,
    )
```
